256 devices in a mesh: section: 8 (over z_lo, core), vocab: 32 (over y, z_hi, x).
Axes of the slice: x: 4, y: 4, z: 8 (z_hi: 2, z_lo: 4; z = z_hi * 4 + z_lo), core: 2. Of those that a mesh axis runs over, the one named last changes fastest.
Arguments:
- hidden: bfloat16 [8, 512, 8192], P('section', None, 'vocab'), may hold values from -160 to 160
- final_hidden: bfloat16 [512, 8192], P('section', 'vocab'), may hold values from -160 to 160
- row_pick: int32 [8, 128], P('section'), may hold values from 0 to 511
- trans_weight: bfloat16 [8, 8192, 8192], P('section', None, 'vocab'), may hold values from -0.0625 to 0.0625
- trans_bias: bfloat16 [8, 8192], P('section', 'vocab'), may hold values from -6 to 6
- norm_gain: bfloat16 [8192], P('vocab'), may hold values from 0.5 to 1.5
- unembed: bfloat16 [8192, 16384], P('section', 'vocab'), may hold values from -100 to 100
Outputs:
- grad_weight: bfloat16 [8, 8192, 8192], P('section', None, 'vocab')
- grad_bias: float32 [8, 8192], P('section', 'vocab')
- kl_mean: float32 [8], P('section')
The draws below stay inside these ranges and needn't reach their ends.
All inputs are finite; a program needn't handle non-finite values.
Results may differ from the reference program's by a relative error of at most 0.024.
Values may be sent and summed in bfloat16 or wider, within the bound.
A program may use at most 64 MiB of HBM per device.

```python
import math
import jax
import jax.numpy as jnp
from jax import lax

D = 8192
ROWS = 128
POOL = 512
VOCAB = 16384
LAYERS = 8


def scaled_field(key, shape):
    base_key, row_key, column_key = jax.random.split(key, 3)
    columns = jnp.exp(jax.random.uniform(column_key, (shape[-1],), jnp.float32, -1.15, 1.15))
    scales = jnp.exp(jax.random.uniform(row_key, shape[:-1] + (1,), jnp.float32, 0.0, 2.3))
    values = jnp.clip(jax.random.normal(base_key, shape, jnp.float32), -5.0, 5.0)
    return jnp.clip(values * columns * scales, -160.0, 160.0).astype(jnp.bfloat16)


def draw_hidden(key, part):
    return scaled_field(jax.random.fold_in(key, 11), (LAYERS, POOL, D))


def draw_final_hidden(key, part):
    return scaled_field(jax.random.fold_in(key, 23), (POOL, D))


def draw_unembed(key, part):
    base_key = jax.random.fold_in(jax.random.fold_in(key, 37), 0)
    spread = 3.0 / math.sqrt(D)
    table = jnp.clip(jax.random.normal(base_key, (D, VOCAB), jnp.float32), -6.0, 6.0) * spread
    return jnp.clip(table, -100.0, 100.0).astype(jnp.bfloat16)


def set_ends(array, stream_key, smallest, top_value):
    extent = array.shape
    spot = [jax.random.randint(jax.random.fold_in(stream_key, axis), (), 0, extent[axis]) for axis in range(len(extent))]
    array = array.at[tuple(spot)].set(smallest)
    longest = extent.index(max(extent))
    spot[longest] = (spot[longest] + 1) % extent[longest]
    return array.at[tuple(spot)].set(top_value)


def level_of(rng, dims, cuts, least, top_value):
    gain, own = 1.0, jax.random.fold_in(rng, 6)
    for position, blocks in cuts:
        steps = jnp.exp(jax.random.uniform(jax.random.fold_in(own, position), (blocks,), jnp.float32, least / len(cuts), top_value / len(cuts)))
        gain = gain * jnp.repeat(steps, dims[position] // blocks).reshape([-1 if axis == position else 1 for axis in range(len(dims))])
    return gain


def gaussian(own_key, extent, width, limit, cuts=(), dtype=jnp.bfloat16):
    array = jax.random.normal(own_key, extent, jnp.float32) * width
    if len(cuts) > 0:
        array = level_of(own_key, extent, cuts, -0.22, 0.18) * array
    return jnp.clip(array, min=-limit, max=limit).astype(dtype)


def setup_inputs(seed: int = 0) -> dict:
    seeds = jax.random.split(jax.random.key(seed), 8)
    hidden = draw_hidden(jax.random.fold_in(seeds[7], 71), 0)
    final_hidden = draw_final_hidden(jax.random.fold_in(seeds[7], 71), 0)
    row_pick = set_ends(jax.random.randint(seeds[2], (LAYERS, ROWS), 0, POOL), jax.random.fold_in(seeds[2], 1), 0, POOL - 1).astype(jnp.int32)
    trans_weight = gaussian(seeds[3], (LAYERS, D, D), D ** -0.5, 0.0625, ((0, 8), (2, 32)))
    trans_bias = gaussian(seeds[4], (LAYERS, D), 1.0, 6.0, ((0, 8), (1, 32)))
    norm_gain = jnp.clip(1.0 + 0.1 * jax.random.normal(seeds[5], (D,), jnp.float32), 0.5, 1.5).astype(jnp.bfloat16)
    unembed = draw_unembed(jax.random.fold_in(seeds[7], 71), 0)
    return dict(hidden=hidden, final_hidden=final_hidden, row_pick=row_pick, trans_weight=trans_weight, trans_bias=trans_bias, norm_gain=norm_gain, unembed=unembed)


epsilon = 1e-05

def log_softmax_rows(values):
    highest = lax.optimization_barrier(jnp.max(values, axis=-1, keepdims=True))
    shifted = values - highest
    return shifted - jnp.log(lax.optimization_barrier(jnp.sum(jnp.exp(shifted), axis=-1, keepdims=True)))

def reference(hidden, final_hidden, row_pick, trans_weight, trans_bias, norm_gain, unembed):
    gain_cols = norm_gain.astype(jnp.float32)
    grad_weights = []
    grad_biases = []
    kl_values = []
    for index_layer in range(LAYERS):
        picked = row_pick[index_layer]
        inputs = hidden[index_layer][picked]
        finals = final_hidden[picked].astype(jnp.float32)
        trans = inputs.astype(jnp.float32) + jnp.dot(inputs, trans_weight[index_layer], preferred_element_type=jnp.float32) + trans_bias[index_layer].astype(jnp.float32)
        trans_scale = lax.rsqrt(lax.optimization_barrier(jnp.mean(trans * trans, axis=-1)) + epsilon)
        final_scale = lax.rsqrt(lax.optimization_barrier(jnp.mean(finals * finals, axis=-1)) + epsilon)
        normed = (trans * trans_scale[:, None] * gain_cols).astype(jnp.bfloat16)
        target = (finals * final_scale[:, None] * gain_cols).astype(jnp.bfloat16)
        log_trans = log_softmax_rows(jnp.dot(normed, unembed, preferred_element_type=jnp.float32))
        log_target = log_softmax_rows(jnp.dot(target, unembed, preferred_element_type=jnp.float32))
        probs = jnp.exp(log_target)
        kl_values.append(jnp.mean(lax.optimization_barrier(jnp.sum(probs * (log_target - log_trans), axis=-1))))
        dlogits = (jnp.exp(log_trans) - probs).astype(jnp.bfloat16)
        dnormed = jnp.dot(dlogits, unembed.T, preferred_element_type=jnp.float32)
        scaled = dnormed * gain_cols
        product = lax.optimization_barrier(jnp.mean(scaled * trans, axis=-1))
        dtrans = trans_scale[:, None] * (scaled - trans * (trans_scale * trans_scale * product)[:, None])
        grad_weights.append(jnp.dot(inputs.T, dtrans.astype(jnp.bfloat16), preferred_element_type=jnp.float32).astype(jnp.bfloat16))
        grad_biases.append(lax.optimization_barrier(jnp.sum(dtrans, axis=0)))
    return (jnp.stack(grad_weights), jnp.stack(grad_biases), jnp.stack(kl_values))
```

```python
import jax
import jax.numpy as jnp
from jax import lax
from jax.experimental import pallas as pl
from jax.experimental.pallas import tpu as pltpu
from jax.sharding import PartitionSpec as P

MESH = pl.DeviceIdType.MESH
F32, BF16 = jnp.float32, jnp.bfloat16
EPS = 1e-05
NV, NS = 32, 8
ROWS, POOL, D, VOC, FB = 128, 512, 8192, 512, 256
VMEM_LIMIT = 60 * 1024 * 1024
N_MSG = 40


def vid(y, x, zh):
    return y * 8 + zh * 4 + x


def ring(a, c):
    return lax.rem(a + (c + 4), 4)


class Place:
    def __init__(self):
        self.v = lax.axis_index("vocab")
        self.s = lax.axis_index("section")
        self.x = lax.rem(self.v, 4)
        self.zh = lax.rem(self.v // 4, 2)
        self.y = self.v // 8
        self.own = self.y * 4 + self.x

    def to(self, v):
        return (self.s, v)

    def partner(self):
        return self.to(vid(self.y, self.x, 1 - self.zh))

    def near(self, half, stage, step):
        along_x = (half == 0) == (stage == 1)
        if along_x:
            return self.to(vid(self.y, ring(self.x, step), self.zh))
        return self.to(vid(ring(self.y, step), self.x, self.zh))

    def pair(self, half, c, d):
        if half == 0:
            return ring(self.y, d) * 4 + ring(self.x, c)
        return ring(self.y, c) * 4 + ring(self.x, d)


def remote(src, dst, send_sem, recv_sem, device):
    return pltpu.make_async_remote_copy(
        src_ref=src, dst_ref=dst, send_sem=send_sem, recv_sem=recv_sem, device_id=device, device_id_type=MESH
    )


def greet(place, sections):
    barrier = pltpu.get_barrier_semaphore()

    @pl.loop(1, NV)
    def _(k):
        pl.semaphore_signal(
            barrier, inc=1, device_id=place.to(lax.rem(place.v + k, NV)), device_id_type=MESH
        )

    if sections:

        @pl.loop(1, NS)
        def _(k):
            pl.semaphore_signal(
                barrier, inc=1, device_id=(lax.rem(place.s + k, NS), place.v), device_id_type=MESH
            )

    pl.semaphore_wait(barrier, NV - 1 + (NS - 1 if sections else 0))


def send_stats(place, stats, send_sem, recv_sem):
    @pl.loop(1, NV)
    def _(k):
        remote(
            stats.at[place.v],
            stats.at[place.v],
            send_sem.at[k],
            recv_sem.at[place.v],
            place.to(lax.rem(place.v + k, NV)),
        ).start()


def wait_stats(place, stats, send_sem, recv_sem):
    @pl.loop(1, NV)
    def _(k):
        src = lax.rem(place.v + k, NV)
        copy = remote(stats.at[src], stats.at[src], send_sem.at[k], recv_sem.at[src], place.to(src))
        copy.wait_send()
        copy.wait_recv()


def to_lanes(columns):
    lane = lax.broadcasted_iota(jnp.int32, (ROWS, 128), 1)
    tile = jnp.zeros((ROWS, 128), F32)
    for k, column in enumerate(columns):
        tile = jnp.where(lane == k, column, tile)
    return tile.T[0:8, :]


def to_columns(tile):
    return jnp.concatenate([tile, jnp.zeros((120, 128), F32)], axis=0).T


class Gather:
    ORDER = (0, -1, 1, 2)

    def __init__(self, place, buf, send_sem, recv_sem):
        self.place, self.buf, self.ss, self.rs = place, buf, send_sem, recv_sem
        self.rows = buf.shape[2]
        self.sent = []
        self.ids = {}

    def span(self, half, part):
        h, q = self.rows // 2, self.rows // 4
        if part == "all":
            return pl.ds(half * h, h)
        return pl.ds(half * h + (0 if part == "first" else q), q)

    def key(self, *name):
        return self.ids.setdefault(name, len(self.ids))

    def move(self, name, pair, half, part, device):
        ref = self.buf.at[pair, :, self.span(half, part), :]
        k = self.key(*name)
        return remote(ref, ref, self.ss.at[k], self.rs.at[k], device)

    def send(self, half, stage, col, c, d, part, step):
        p = self.place
        copy = self.move((half, stage, col, part, step), p.pair(half, c, d), half, part, p.near(half, stage, step))
        copy.start()
        self.sent.append(copy)

    def wait(self, half, stage, col, c, d, part, step):
        p = self.place
        self.move((half, stage, col, part, step), p.pair(half, c, d), half, part, p.near(half, stage, -step)).wait_recv()

    def partner(self, zsend, zrecv):
        p = self.place
        mine = self.buf.at[p.own, p.zh]
        return (
            remote(mine, mine, zsend, zrecv, p.partner()),
            remote(self.buf.at[p.own, 1 - p.zh], self.buf.at[p.own, 1 - p.zh], zsend, zrecv, p.partner()),
        )

    def run(self, zsend, zrecv):
        out, back = self.partner(zsend, zrecv)
        out.start()
        back.wait_recv()
        for half in (0, 1):
            for step in (1, -1):
                self.send(half, 1, 0, 0, 0, "all", step)
        for half in (0, 1):
            for step in (1, -1):
                self.send(half, 2, 0, 0, 0, "all", step)
        for step, part in ((1, "first"), (-1, "second")):
            for half in (0, 1):
                self.wait(half, 1, 0, -step, 0, "all", step)
                self.send(half, 1, 0, -step, 0, part, step)
                for turn in (1, -1):
                    self.send(half, 2, -step, -step, 0, "all", turn)
        for step, part in ((1, "first"), (-1, "second")):
            for half in (0, 1):
                self.wait(half, 2, 0, 0, -step, "all", step)
                self.send(half, 2, 0, 0, -step, part, step)
        for half in (0, 1):
            self.wait(half, 1, 0, 2, 0, "first", 1)
            self.wait(half, 1, 0, 2, 0, "second", -1)
            for turn in (1, -1):
                self.send(half, 2, 2, 2, 0, "all", turn)
        for c in (-1, 1, 2):
            for step, part in ((1, "first"), (-1, "second")):
                for half in (0, 1):
                    self.wait(half, 2, c, c, -step, "all", step)
                    self.send(half, 2, c, c, -step, part, step)
        for c in self.ORDER:
            for half in (0, 1):
                self.wait(half, 2, c, c, 2, "first", 1)
                self.wait(half, 2, c, c, 2, "second", -1)
        out.wait_send()
        for copy in self.sent:
            copy.wait_send()


def kernel_a(
    pick, hidden, final, w_hbm, bias, gain, x_out, lt_out, trans_out, scale_out,
    xbuf, ltbuf, fbuf, wbuf, stats, acc, w_sem, o_sem, fs, fr, zs, zr, ss1, rs1, ss2, rs2, sts, str_,
):
    place = Place()
    w_copy = pltpu.make_async_copy(w_hbm, wbuf, w_sem)
    w_copy.start()
    onehot = jnp.where(lax.broadcasted_iota(jnp.int32, (ROWS, POOL), 1) == pick[...], 1.0, 0.0).astype(BF16)
    inputs = jnp.dot(onehot, hidden[...], preferred_element_type=F32)
    xbuf[place.own, place.zh] = inputs.astype(BF16)
    greet(place, True)

    @pl.loop(1, NS)
    def _(k):
        remote(
            final, fbuf.at[place.s], fs.at[k], fr.at[place.s], (lax.rem(place.s + k, NS), place.v)
        ).start()

    fbuf[place.s] = final[...]
    Gather(place, xbuf, ss1, rs1).run(zs.at[0], zr.at[0])
    x_copy = pltpu.make_async_copy(xbuf, x_out, o_sem.at[0])
    x_copy.start()

    @pl.loop(1, NS)
    def _(k):
        src = lax.rem(place.s + k, NS)
        copy = remote(fbuf.at[src], fbuf.at[src], fs.at[k], fr.at[src], (src, place.v))
        copy.wait_send()
        copy.wait_recv()

    finals = jnp.dot(onehot, fbuf[...].reshape(POOL, FB), preferred_element_type=F32)
    w_copy.wait()
    acc[...] = xbuf[place.own, place.zh].astype(F32) + bias[...].astype(F32)

    @pl.loop(0, 16)
    def _(p):
        y, x = p // 4, lax.rem(p, 4)
        total = acc[...]
        for zh in (0, 1):
            rows = pl.ds(pl.multiple_of(vid(y, x, zh) * FB, FB), FB)
            total = total + jnp.dot(xbuf[p, zh], wbuf[rows, :], preferred_element_type=F32)
        acc[...] = total

    trans = acc[...]
    gain_cols = gain[...].astype(F32)
    ltbuf[place.own, place.zh, 0:ROWS] = (trans * gain_cols).astype(BF16)
    ltbuf[place.own, place.zh, ROWS : 2 * ROWS] = (finals * gain_cols).astype(BF16)
    stats[place.v] = to_lanes(
        [jnp.sum(trans * trans, axis=1, keepdims=True), jnp.sum(finals * finals, axis=1, keepdims=True)]
    )
    trans_out[...] = trans
    send_stats(place, stats, sts, str_)
    Gather(place, ltbuf, ss2, rs2).run(zs.at[1], zr.at[1])
    lt_copy = pltpu.make_async_copy(ltbuf, lt_out, o_sem.at[1])
    lt_copy.start()
    wait_stats(place, stats, sts, str_)
    scale_out[...] = lax.rsqrt(jnp.sum(stats[...], axis=0) / D + EPS)
    x_copy.wait()
    lt_copy.wait()


def kernel_b(
    lt_hbm, u_hbm, trans, scale, gain, dtrans_out, bias_out, kl_out,
    lt, u, acc, stats, part, sbuf, rq, rp, rm, r1p, r1m, rz, in_sem, sts, str_, ss, rs, zs, zr,
):
    place = Place()
    chunk = D // 8
    lt_copy = pltpu.make_async_copy(lt_hbm, lt, in_sem.at[8])
    lt_copy.start()
    u_copies = []
    for i in range(8):
        rows = pl.ds(i * chunk, chunk)
        u_copies.append(pltpu.make_async_copy(u_hbm.at[rows], u.at[rows], in_sem.at[i]))
        u_copies[-1].start()
    greet(place, False)
    lt_copy.wait()
    for i in range(8):
        u_copies[i].wait()
        total = acc[...] if i > 0 else None
        for v in range(4 * i, 4 * i + 4):
            p, zh = (v // 8) * 4 + v % 4, (v // 4) % 2
            term = jnp.dot(lt[p, zh], u[v * FB : (v + 1) * FB, :], preferred_element_type=F32)
            total = term if total is None else total + term
        acc[...] = total
    columns = to_columns(scale[...])
    trans_scale, final_scale = columns[:, 0:1], columns[:, 1:2]
    logits = acc[0:ROWS] * trans_scale
    target = acc[ROWS : 2 * ROWS] * final_scale

    def totals(values):
        highest = jnp.max(values, axis=1, keepdims=True)
        shifted = values - highest
        weights = jnp.exp(shifted)
        return highest, shifted, weights, jnp.sum(weights, axis=1, keepdims=True)

    l_max, l_shift, l_exp, l_sum = totals(logits)
    t_max, t_shift, t_exp, t_sum = totals(target)
    stats[place.v] = to_lanes(
        [
            l_max,
            l_sum,
            jnp.sum(l_exp * l_shift, axis=1, keepdims=True),
            t_max,
            t_sum,
            jnp.sum(t_exp * t_shift, axis=1, keepdims=True),
            jnp.sum(t_exp * l_shift, axis=1, keepdims=True),
        ]
    )
    send_stats(place, stats, sts, str_)
    wait_stats(place, stats, sts, str_)
    lm, ls, la, tm, ts, ta, tb = (stats[:, k, :] for k in range(7))

    def over(values):
        return jnp.sum(values, axis=0, keepdims=True)

    l_top = jnp.max(lm, axis=0, keepdims=True)
    t_top = jnp.max(tm, axis=0, keepdims=True)
    lw, tw = jnp.exp(lm - l_top), jnp.exp(tm - t_top)
    l_total, t_total = over(lw * ls), over(tw * ts)
    mean_l = over(lw * (la + ls * (lm - l_top))) / l_total
    mean_t = over(tw * (ta + ts * (tm - t_top))) / t_total
    mean_tl = over(tw * (tb + ts * (lm - l_top))) / t_total
    kl_rows = mean_t - mean_tl - jnp.log(t_total) + jnp.log(l_total)
    kl_out[...] = jnp.broadcast_to(jnp.sum(kl_rows, axis=1, keepdims=True) / ROWS, (8, 128))
    l_norm = l_top + jnp.log(l_total)
    t_norm = t_top + jnp.log(t_total)
    pull = scale[0:1, :] * (mean_l - mean_tl) / D
    columns = to_columns(jnp.concatenate([l_norm, t_norm, pull, jnp.zeros((5, 128), F32)], axis=0))
    l_norm, t_norm, pull = columns[:, 0:1], columns[:, 1:2], columns[:, 2:3]
    dlogits = (jnp.exp(logits - l_norm) - jnp.exp(target - t_norm)).astype(BF16)

    ids = {}
    sent = []
    half_rows, quarter = ROWS // 2, ROWS // 4

    def span(half, name):
        if name == "all":
            return pl.ds(half * half_rows, half_rows)
        return pl.ds(half * half_rows + (0 if name == "first" else quarter), quarter)

    def product(pair):
        y, x = pair // 4, lax.rem(pair, 4)
        for zh in (0, 1):
            rows = pl.ds(pl.multiple_of(vid(y, x, zh) * FB, FB), FB)
            part[pair, zh] = lax.dot_general(
                dlogits, u[rows, :], (((1,), (1,)), ((), ())), preferred_element_type=F32
            )

    def move(name, src, dst, device):
        k = ids.setdefault(name, len(ids))
        return remote(src, dst, ss.at[k], rs.at[k], device)

    def landing(stage, name, step, pair, half):
        rows = span(half, name)
        if name != "all":
            return rq.at[pair, :, rows, :]
        if stage == 2:
            return (rp if step == 1 else rm).at[pair, :, rows, :]
        return (r1p if step == 1 else r1m).at[:, rows, :]

    def send(half, stage, col, c, d, name, step):
        pair = place.pair(half, c, d)
        copy = move(
            (half, stage, col, name, step),
            sbuf.at[pair, :, span(half, name), :],
            landing(stage, name, step, pair, half),
            place.near(half, stage, step),
        )
        copy.start()
        sent.append(copy)

    def receive(half, stage, col, c, d, name, step):
        pair = place.pair(half, c, d)
        ref = landing(stage, name, step, pair, half)
        move((half, stage, col, name, step), ref, ref, place.near(half, stage, -step)).wait_recv()
        return ref[...].astype(F32)

    def put(half, c, d, name, value):
        sbuf[place.pair(half, c, d), :, span(half, name), :] = value.astype(BF16)

    def mine(half, c, d, name):
        return part[place.pair(half, c, d), :, span(half, name), :]

    first = [(2, 2)] + [(2, k) for k in (-1, 1, 0)] + [(k, 2) for k in (-1, 1, 0)]
    later = [(-1, -1), (-1, 1), (1, -1), (1, 1), (0, -1), (0, 1), (-1, 0), (1, 0), (0, 0)]
    for dx, dy in first:
        product(place.pair(0, dx, dy))
        for half in (0, 1):
            c, d = (dx, dy) if half == 0 else (dy, dx)
            if d == 2:
                put(half, c, 2, "all", mine(half, c, 2, "all"))
                send(half, 2, c, c, 2, "first", -1)
                send(half, 2, c, c, 2, "second", 1)
    for dx, dy in later:
        product(place.pair(0, dx, dy))
    order = (2, -1, 1, 0)
    for c in order:
        for half in (0, 1):
            for step, name in ((-1, "first"), (1, "second")):
                arrived = receive(half, 2, c, c, step, name, step)
                put(half, c, step, "all", mine(half, c, step, "all"))
                put(half, c, step, name, mine(half, c, step, name) + arrived)
                send(half, 2, c, c, step, "all", step)
    own_sum = [None, None]
    for c in order:
        for half in (0, 1):
            total = mine(half, c, 0, "all")
            for step in (1, -1):
                total = total + receive(half, 2, c, c, 0, "all", step)
            if c == 2:
                put(half, 2, 0, "all", total)
                send(half, 1, 0, 2, 0, "first", -1)
                send(half, 1, 0, 2, 0, "second", 1)
            elif c != 0:
                name = "first" if c == -1 else "second"
                arrived = receive(half, 1, 0, c, 0, name, c)
                zero = jnp.zeros_like(arrived)
                pieces = [arrived, zero] if name == "first" else [zero, arrived]
                put(half, c, 0, "all", total + jnp.concatenate(pieces, axis=1))
                send(half, 1, 0, c, 0, "all", c)
            else:
                for step in (1, -1):
                    total = total + receive(half, 1, 0, 0, 0, "all", step)
                put(half, 0, 0, "all", total)
                part[place.own, :, span(half, "all"), :] = total
    out = remote(sbuf.at[place.own, 1 - place.zh], rz, zs, zr, place.partner())
    out.start()
    out.wait_recv()
    dnormed = part[place.own, place.zh] + rz[...].astype(F32)
    scaled = dnormed * gain[...].astype(F32)
    dtrans = trans_scale * (scaled - trans[...] * pull)
    dtrans_out[...] = dtrans.astype(BF16)
    bias_out[...] = jnp.sum(dtrans, axis=0, keepdims=True)
    out.wait_send()
    for copy in sent:
        copy.wait_send()


def kernel_c(x, dtrans, out):
    out[...] = lax.dot_general(
        x[0, 0], dtrans[...], (((0,), (0,)), ((), ())), preferred_element_type=F32
    ).astype(BF16)


def per_device(hidden, final_hidden, row_pick, trans_weight, trans_bias, norm_gain, unembed):
    unembed_full = lax.all_gather(unembed, "section", axis=0, tiled=True)
    whole = pl.BlockSpec(memory_space=pltpu.VMEM)
    anywhere = pl.BlockSpec(memory_space=pl.ANY)
    dma = pltpu.SemaphoreType.DMA
    gain = norm_gain.reshape(1, FB)
    shape = jax.ShapeDtypeStruct
    x_all, lt_all, trans, scale = pl.pallas_call(
        kernel_a,
        name="gather_rows",
        out_shape=(
            shape((16, 2, ROWS, FB), BF16),
            shape((16, 2, 2 * ROWS, FB), BF16),
            shape((ROWS, FB), F32),
            shape((8, 128), F32),
        ),
        in_specs=[whole, whole, whole, anywhere, whole, whole],
        out_specs=(anywhere, anywhere, whole, whole),
        scratch_shapes=[
            pltpu.VMEM((16, 2, ROWS, FB), BF16),
            pltpu.VMEM((16, 2, 2 * ROWS, FB), BF16),
            pltpu.VMEM((NS, POOL // NS, FB), BF16),
            pltpu.VMEM((D, FB), BF16),
            pltpu.VMEM((NV, 8, 128), F32),
            pltpu.VMEM((ROWS, FB), F32),
            dma,
            dma((2,)),
            dma((NS,)),
            dma((NS,)),
            dma((2,)),
            dma((2,)),
            dma((N_MSG,)),
            dma((N_MSG,)),
            dma((N_MSG,)),
            dma((N_MSG,)),
            dma((NV,)),
            dma((NV,)),
        ],
        compiler_params=pltpu.CompilerParams(
            collective_id=0, has_side_effects=True, vmem_limit_bytes=VMEM_LIMIT
        ),
        cost_estimate=pl.CostEstimate(flops=10**9, bytes_accessed=10**8, transcendentals=0),
    )(row_pick.reshape(ROWS, 1), hidden[0], final_hidden, trans_weight[0], trans_bias, gain)
    dtrans, grad_bias, kl = pl.pallas_call(
        kernel_b,
        name="softmax_scatter",
        out_shape=(shape((ROWS, FB), BF16), shape((1, FB), F32), shape((8, 128), F32)),
        in_specs=[anywhere, anywhere, whole, whole, whole],
        out_specs=(whole, whole, whole),
        scratch_shapes=[
            pltpu.VMEM((16, 2, 2 * ROWS, FB), BF16),
            pltpu.VMEM((D, VOC), BF16),
            pltpu.VMEM((2 * ROWS, VOC), F32),
            pltpu.VMEM((NV, 8, 128), F32),
            pltpu.VMEM((16, 2, ROWS, FB), F32),
            pltpu.VMEM((16, 2, ROWS, FB), BF16),
            pltpu.VMEM((16, 2, ROWS, FB), BF16),
            pltpu.VMEM((16, 2, ROWS, FB), BF16),
            pltpu.VMEM((16, 2, ROWS, FB), BF16),
            pltpu.VMEM((2, ROWS, FB), BF16),
            pltpu.VMEM((2, ROWS, FB), BF16),
            pltpu.VMEM((ROWS, FB), BF16),
            dma((9,)),
            dma((NV,)),
            dma((NV,)),
            dma((N_MSG,)),
            dma((N_MSG,)),
            dma,
            dma,
        ],
        compiler_params=pltpu.CompilerParams(
            collective_id=1, has_side_effects=True, vmem_limit_bytes=VMEM_LIMIT
        ),
        cost_estimate=pl.CostEstimate(flops=10**9, bytes_accessed=10**8, transcendentals=0),
    )(lt_all, unembed_full, trans, scale, gain)
    grad_weight = pl.pallas_call(
        kernel_c,
        name="weight_gradient",
        grid=(NV,),
        out_shape=shape((D, FB), BF16),
        in_specs=[
            pl.BlockSpec((1, 1, ROWS, FB), lambda v: ((v // 8) * 4 + v % 4, (v // 4) % 2, 0, 0)),
            pl.BlockSpec((ROWS, FB), lambda v: (0, 0)),
        ],
        out_specs=pl.BlockSpec((FB, FB), lambda v: (v, 0)),
    )(x_all, dtrans)
    return grad_weight[None], grad_bias, kl[0, 0:1]


def solution(mesh):
    placed = (
        P("section", None, "vocab"),
        P("section", "vocab"),
        P("section", None),
        P("section", None, "vocab"),
        P("section", "vocab"),
        P("vocab"),
        P("section", "vocab"),
    )
    return jax.shard_map(
        per_device,
        mesh=mesh,
        in_specs=placed,
        out_specs=(P("section", None, "vocab"), P("section", "vocab"), P("section")),
        check_vma=False,
    )
```

```python
import jax
import jax.numpy as jnp
from jax import lax
from jax.experimental import pallas as pl
from jax.experimental.pallas import tpu as pltpu
from jax.sharding import PartitionSpec as P

MESH = pl.DeviceIdType.MESH
F32, BF16 = jnp.float32, jnp.bfloat16
EPS = 1e-05
NV, NS = 32, 8
ROWS, POOL, D, VOC, FB = 128, 512, 8192, 512, 256
VMEM_LIMIT = 60 * 1024 * 1024
N_MSG = 40
CHUNKS = 2
SHARD = D // NS
PIECE = SHARD // CHUNKS


def vid(y, x, zh):
    return y * 8 + zh * 4 + x


def ring(a, c):
    return lax.rem(a + (c + 4), 4)


class Place:
    def __init__(self):
        self.v = lax.axis_index("vocab")
        self.s = lax.axis_index("section")
        self.x = lax.rem(self.v, 4)
        self.zh = lax.rem(self.v // 4, 2)
        self.y = self.v // 8
        self.own = self.y * 4 + self.x

    def to(self, v):
        return (self.s, v)

    def partner(self):
        return self.to(vid(self.y, self.x, 1 - self.zh))

    def near(self, half, stage, step):
        along_x = (half == 0) == (stage == 1)
        if along_x:
            return self.to(vid(self.y, ring(self.x, step), self.zh))
        return self.to(vid(ring(self.y, step), self.x, self.zh))

    def pair(self, half, c, d):
        if half == 0:
            return ring(self.y, d) * 4 + ring(self.x, c)
        return ring(self.y, c) * 4 + ring(self.x, d)


def remote(src, dst, send_sem, recv_sem, device):
    return pltpu.make_async_remote_copy(
        src_ref=src, dst_ref=dst, send_sem=send_sem, recv_sem=recv_sem, device_id=device, device_id_type=MESH
    )


def greet(place):
    barrier = pltpu.get_barrier_semaphore()

    @pl.loop(1, NV)
    def _(k):
        pl.semaphore_signal(
            barrier, inc=1, device_id=place.to(lax.rem(place.v + k, NV)), device_id_type=MESH
        )

    @pl.loop(1, NS)
    def _(k):
        pl.semaphore_signal(
            barrier, inc=1, device_id=(lax.rem(place.s + k, NS), place.v), device_id_type=MESH
        )

    pl.semaphore_wait(barrier, NV - 1 + NS - 1)


def send_stats(place, stats, send_sem, recv_sem):
    @pl.loop(1, NV)
    def _(k):
        remote(
            stats.at[place.v],
            stats.at[place.v],
            send_sem.at[k],
            recv_sem.at[place.v],
            place.to(lax.rem(place.v + k, NV)),
        ).start()


def wait_stats(place, stats, send_sem, recv_sem):
    @pl.loop(1, NV)
    def _(k):
        src = lax.rem(place.v + k, NV)
        copy = remote(stats.at[src], stats.at[src], send_sem.at[k], recv_sem.at[src], place.to(src))
        copy.wait_send()
        copy.wait_recv()


def to_lanes(columns):
    lane = lax.broadcasted_iota(jnp.int32, (ROWS, 128), 1)
    tile = jnp.zeros((ROWS, 128), F32)
    for k, column in enumerate(columns):
        tile = jnp.where(lane == k, column, tile)
    return tile.T[0:8, :]


def to_columns(tile):
    return jnp.concatenate([tile, jnp.zeros((120, 128), F32)], axis=0).T


class Gather:
    ORDER = (0, -1, 1, 2)

    def __init__(self, place, buf, send_sem, recv_sem):
        self.place, self.buf, self.ss, self.rs = place, buf, send_sem, recv_sem
        self.rows = buf.shape[2]
        self.sent = []
        self.ids = {}

    def span(self, half, part):
        h, q = self.rows // 2, self.rows // 4
        if part == "all":
            return pl.ds(half * h, h)
        return pl.ds(half * h + (0 if part == "first" else q), q)

    def key(self, *name):
        return self.ids.setdefault(name, len(self.ids))

    def move(self, name, pair, half, part, device):
        ref = self.buf.at[pair, :, self.span(half, part), :]
        k = self.key(*name)
        return remote(ref, ref, self.ss.at[k], self.rs.at[k], device)

    def send(self, half, stage, col, c, d, part, step):
        p = self.place
        copy = self.move((half, stage, col, part, step), p.pair(half, c, d), half, part, p.near(half, stage, step))
        copy.start()
        self.sent.append(copy)

    def wait(self, half, stage, col, c, d, part, step):
        p = self.place
        self.move((half, stage, col, part, step), p.pair(half, c, d), half, part, p.near(half, stage, -step)).wait_recv()

    def partner(self, zsend, zrecv):
        p = self.place
        mine = self.buf.at[p.own, p.zh]
        return (
            remote(mine, mine, zsend, zrecv, p.partner()),
            remote(self.buf.at[p.own, 1 - p.zh], self.buf.at[p.own, 1 - p.zh], zsend, zrecv, p.partner()),
        )

    def run(self, zsend, zrecv, hooks):
        def reach(point):
            if point in hooks:
                hooks[point]()

        out, back = self.partner(zsend, zrecv)
        out.start()
        reach("start")
        back.wait_recv()
        for half in (0, 1):
            for step in (1, -1):
                self.send(half, 1, 0, 0, 0, "all", step)
        for half in (0, 1):
            for step in (1, -1):
                self.send(half, 2, 0, 0, 0, "all", step)
        reach("sent")
        for step, part in ((1, "first"), (-1, "second")):
            for half in (0, 1):
                self.wait(half, 1, 0, -step, 0, "all", step)
                self.send(half, 1, 0, -step, 0, part, step)
                for turn in (1, -1):
                    self.send(half, 2, -step, -step, 0, "all", turn)
        for step, part in ((1, "first"), (-1, "second")):
            for half in (0, 1):
                self.wait(half, 2, 0, 0, -step, "all", step)
                self.send(half, 2, 0, 0, -step, part, step)
        for half in (0, 1):
            self.wait(half, 1, 0, 2, 0, "first", 1)
            self.wait(half, 1, 0, 2, 0, "second", -1)
            for turn in (1, -1):
                self.send(half, 2, 2, 2, 0, "all", turn)
        reach("turned")
        for c in (-1, 1, 2):
            for step, part in ((1, "first"), (-1, "second")):
                for half in (0, 1):
                    self.wait(half, 2, c, c, -step, "all", step)
                    self.send(half, 2, c, c, -step, part, step)
        for c in self.ORDER:
            for half in (0, 1):
                self.wait(half, 2, c, c, 2, "first", 1)
                self.wait(half, 2, c, c, 2, "second", -1)
        out.wait_send()

    def drain(self):
        for copy in self.sent:
            copy.wait_send()


class Table:
    def __init__(self, place, mine, buf, to_z, to_core, arrived, local):
        self.place, self.mine, self.buf = place, mine, buf
        self.to_z, self.to_core, self.arrived, self.local = to_z, to_core, arrived, local
        self.core = lax.rem(place.s, 2)
        self.zl = place.s // 2

    def piece(self, shard, part):
        return self.buf.at[shard, pl.ds(part * PIECE, PIECE), :]

    def along(self, i, part, sign, src=None):
        shard = 2 * i + self.core
        here = self.piece(shard, part) if src is None else src
        return remote(
            here,
            self.piece(shard, part),
            self.to_z.at[0 if sign > 0 else 1, i, part],
            self.arrived.at[shard, part],
            (self.place.s + 2 * sign, self.place.v),
        )

    def across(self, i, part, src=None):
        shard = 2 * i + self.core
        here = self.piece(shard, part) if src is None else src
        return remote(
            here,
            self.piece(shard, part),
            self.to_core.at[i, part],
            self.arrived.at[shard, part],
            (self.place.s + 1 - 2 * self.core, self.place.v),
        )

    def start(self):
        for part in range(CHUNKS):
            src = self.mine.at[pl.ds(part * PIECE, PIECE), :]

            @pl.when(self.zl < 3)
            def _():
                self.along(self.zl, part, 1, src).start()

            @pl.when(self.zl > 0)
            def _():
                self.along(self.zl, part, -1, src).start()

        for part in range(CHUNKS):
            self.across(self.zl, part, self.mine.at[pl.ds(part * PIECE, PIECE), :]).start()
        pltpu.make_async_copy(self.mine, self.buf.at[self.place.s], self.local).start()

    def wait(self, shard, part):
        ref = self.piece(shard, part)
        remote(ref, ref, self.to_core.at[0, part], self.arrived.at[shard, part], (self.place.s, self.place.v)).wait_recv()

    def relay(self, wave, part):
        for side in (-1, 1):
            i = self.zl + side * wave
            beyond = self.zl - side

            @pl.when((i >= 0) & (i <= 3))
            def _():
                self.wait(2 * i + self.core, part)

                @pl.when((beyond >= 0) & (beyond <= 3))
                def _():
                    self.along(i, part, -side).start()

                self.across(i, part).start()

    def drain(self):
        for part in range(CHUNKS):
            for i in range(4):

                @pl.when((self.zl < 3) & (self.zl >= i))
                def _():
                    self.along(i, part, 1).wait_send()

                @pl.when((self.zl > 0) & (self.zl <= i))
                def _():
                    self.along(i, part, -1).wait_send()

                self.across(i, part).wait_send()


def kernel(
    pick, hidden, final, w_hbm, bias, gain, u_mine, x_out, dtrans_out, kl_out,
    xbuf, lt, fbuf, wbuf, u, trans_ref, acc, scale_stats, stats, part, sbuf, rq, rp, rm, r1p, r1m, rz,
    w_sem, x_sem, u_sem, uz, uc, ua, fs, fr, zs, zr, ss1, rs1, ss2, rs2, ss, rs, sts1, str1, sts2, str2,
):
    place = Place()
    table = Table(place, u_mine, u, uz, uc, ua, u_sem)
    w_copy = pltpu.make_async_copy(w_hbm, wbuf, w_sem)
    w_copy.start()
    chosen = jnp.broadcast_to(pick[...].astype(F32), (ROWS, ROWS)).T[:, 0:1].astype(jnp.int32)
    onehot = jnp.where(lax.broadcasted_iota(jnp.int32, (ROWS, POOL), 1) == chosen, 1.0, 0.0).astype(BF16)
    inputs = jnp.dot(onehot, hidden[...], preferred_element_type=F32)
    xbuf[place.own, place.zh] = inputs.astype(BF16)
    greet(place)

    def begin():
        @pl.loop(1, NS)
        def _(k):
            remote(
                final, fbuf.at[place.s], fs.at[k], fr.at[place.s], (lax.rem(place.s + k, NS), place.v)
            ).start()

        table.start()
        fbuf[place.s] = final[...]

    gather_x = Gather(place, xbuf, ss1, rs1)
    gather_x.run(zs.at[0], zr.at[0], {"start": begin, "turned": lambda: table.relay(1, 0)})
    x_copy = pltpu.make_async_copy(xbuf, x_out, x_sem)
    x_copy.start()

    @pl.loop(1, NS)
    def _(k):
        src = lax.rem(place.s + k, NS)
        copy = remote(fbuf.at[src], fbuf.at[src], fs.at[k], fr.at[src], (src, place.v))
        copy.wait_send()
        copy.wait_recv()

    finals = jnp.dot(onehot, fbuf[...].reshape(POOL, FB), preferred_element_type=F32)
    w_copy.wait()
    gain_cols = gain[...].astype(F32).reshape(1, FB)
    trans_ref[...] = xbuf[place.own, place.zh].astype(F32) + bias[...].astype(F32)

    @pl.loop(0, 16)
    def _(p):
        y, x = p // 4, lax.rem(p, 4)
        total = trans_ref[...]
        for zh in (0, 1):
            rows = pl.ds(pl.multiple_of(vid(y, x, zh) * FB, FB), FB)
            total = total + jnp.dot(xbuf[p, zh], wbuf[rows, :], preferred_element_type=F32)
        trans_ref[...] = total

    trans = trans_ref[...]
    lt[place.own, place.zh, 0:ROWS] = (trans * gain_cols).astype(BF16)
    lt[place.own, place.zh, ROWS : 2 * ROWS] = (finals * gain_cols).astype(BF16)
    scale_stats[place.v] = to_lanes(
        [jnp.sum(trans * trans, axis=1, keepdims=True), jnp.sum(finals * finals, axis=1, keepdims=True)]
    )
    send_stats(place, scale_stats, sts1, str1)
    gather_lt = Gather(place, lt, ss2, rs2)
    gather_lt.run(
        zs.at[1], zr.at[1], {"sent": lambda: table.relay(1, 1), "turned": lambda: table.relay(2, 0)}
    )
    table.relay(2, 1)
    acc[...] = jnp.zeros_like(acc)

    def absorb(shard, first, count):
        total = acc[...]
        for k in range(first, first + count):
            total = total + jnp.dot(
                lt[(shard // 2) * 4 + k, lax.rem(shard, 2)],
                u[shard, k * FB : (k + 1) * FB, :],
                preferred_element_type=F32,
            )
        acc[...] = total

    pltpu.make_async_copy(u_mine, u.at[place.s], u_sem).wait()
    absorb(place.s, 0, 4)
    other = place.s + 1 - 2 * table.core
    for piece in range(CHUNKS):
        table.wait(other, piece)
    absorb(other, 0, 4)
    for wave in (1, 2, 3):
        for piece in range(CHUNKS):
            if wave == 3:
                table.relay(3, piece)
            for side in (-1, 1):
                i = table.zl + side * wave

                @pl.when((i >= 0) & (i <= 3))
                def _():
                    per = 4 // CHUNKS
                    absorb(2 * i + table.core, piece * per, per)
                    table.wait(2 * i + 1 - table.core, piece)
                    absorb(2 * i + 1 - table.core, piece * per, per)

    wait_stats(place, scale_stats, sts1, str1)
    scale = lax.rsqrt(jnp.sum(scale_stats[...], axis=0) / D + EPS)


    columns = to_columns(scale)
    trans_scale, final_scale = columns[:, 0:1], columns[:, 1:2]
    logits = acc[0:ROWS] * trans_scale
    target = acc[ROWS : 2 * ROWS] * final_scale

    def totals(values):
        highest = jnp.max(values, axis=1, keepdims=True)
        shifted = values - highest
        weights = jnp.exp(shifted)
        return highest, shifted, weights, jnp.sum(weights, axis=1, keepdims=True)

    l_max, l_shift, l_exp, l_sum = totals(logits)
    t_max, t_shift, t_exp, t_sum = totals(target)
    stats[place.v] = to_lanes(
        [
            l_max,
            l_sum,
            jnp.sum(l_exp * l_shift, axis=1, keepdims=True),
            t_max,
            t_sum,
            jnp.sum(t_exp * t_shift, axis=1, keepdims=True),
            jnp.sum(t_exp * l_shift, axis=1, keepdims=True),
        ]
    )
    send_stats(place, stats, sts2, str2)
    wait_stats(place, stats, sts2, str2)
    lm, ls, la, tm, ts, ta, tb = (stats[:, k, :] for k in range(7))

    def over(values):
        return jnp.sum(values, axis=0, keepdims=True)

    l_top = jnp.max(lm, axis=0, keepdims=True)
    t_top = jnp.max(tm, axis=0, keepdims=True)
    lw, tw = jnp.exp(lm - l_top), jnp.exp(tm - t_top)
    l_total, t_total = over(lw * ls), over(tw * ts)
    mean_l = over(lw * (la + ls * (lm - l_top))) / l_total
    mean_t = over(tw * (ta + ts * (tm - t_top))) / t_total
    mean_tl = over(tw * (tb + ts * (lm - l_top))) / t_total
    kl_rows = mean_t - mean_tl - jnp.log(t_total) + jnp.log(l_total)
    kl_out[...] = kl_rows
    l_norm = l_top + jnp.log(l_total)
    t_norm = t_top + jnp.log(t_total)
    pull = scale[0:1, :] * (mean_l - mean_tl) / D
    columns = to_columns(jnp.concatenate([l_norm, t_norm, pull, jnp.zeros((5, 128), F32)], axis=0))
    l_norm, t_norm, pull = columns[:, 0:1], columns[:, 1:2], columns[:, 2:3]
    dlogits = (jnp.exp(logits - l_norm) - jnp.exp(target - t_norm)).astype(BF16)

    ids = {}
    sent = []
    half_rows, quarter = ROWS // 2, ROWS // 4

    def span(half, name):
        if name == "all":
            return pl.ds(half * half_rows, half_rows)
        return pl.ds(half * half_rows + (0 if name == "first" else quarter), quarter)

    def product(pair):
        y, x = pair // 4, lax.rem(pair, 4)
        for zh in (0, 1):
            rows = pl.ds(pl.multiple_of(x * FB, FB), FB)
            part[pair, zh] = lax.dot_general(
                dlogits, u[2 * y + zh, rows, :], (((1,), (1,)), ((), ())), preferred_element_type=F32
            )

    def move(name, src, dst, device):
        k = ids.setdefault(name, len(ids))
        return remote(src, dst, ss.at[k], rs.at[k], device)

    def landing(stage, name, step, pair, half):
        rows = span(half, name)
        if name != "all":
            return rq.at[pair, :, rows, :]
        if stage == 2:
            return (rp if step == 1 else rm).at[pair, :, rows, :]
        return (r1p if step == 1 else r1m).at[:, rows, :]

    def send(half, stage, col, c, d, name, step):
        pair = place.pair(half, c, d)
        copy = move(
            (half, stage, col, name, step),
            sbuf.at[pair, :, span(half, name), :],
            landing(stage, name, step, pair, half),
            place.near(half, stage, step),
        )
        copy.start()
        sent.append(copy)

    def receive(half, stage, col, c, d, name, step):
        pair = place.pair(half, c, d)
        ref = landing(stage, name, step, pair, half)
        move((half, stage, col, name, step), ref, ref, place.near(half, stage, -step)).wait_recv()
        return ref[...].astype(F32)

    def put(half, c, d, name, value):
        sbuf[place.pair(half, c, d), :, span(half, name), :] = value.astype(BF16)

    def mine(half, c, d, name):
        return part[place.pair(half, c, d), :, span(half, name), :]

    first = [(2, 2)] + [(2, k) for k in (-1, 1, 0)] + [(k, 2) for k in (-1, 1, 0)]
    later = [(-1, -1), (-1, 1), (1, -1), (1, 1), (0, -1), (0, 1), (-1, 0), (1, 0), (0, 0)]
    for dx, dy in first:
        product(place.pair(0, dx, dy))
        for half in (0, 1):
            c, d = (dx, dy) if half == 0 else (dy, dx)
            if d == 2:
                put(half, c, 2, "all", mine(half, c, 2, "all"))
                send(half, 2, c, c, 2, "first", -1)
                send(half, 2, c, c, 2, "second", 1)
    for dx, dy in later:
        product(place.pair(0, dx, dy))
    order = (2, -1, 1, 0)
    for c in order:
        for half in (0, 1):
            for step, name in ((-1, "first"), (1, "second")):
                arrived = receive(half, 2, c, c, step, name, step)
                put(half, c, step, "all", mine(half, c, step, "all"))
                put(half, c, step, name, mine(half, c, step, name) + arrived)
                send(half, 2, c, c, step, "all", step)
    own_sum = [None, None]
    for c in order:
        for half in (0, 1):
            total = mine(half, c, 0, "all")
            for step in (1, -1):
                total = total + receive(half, 2, c, c, 0, "all", step)
            if c == 2:
                put(half, 2, 0, "all", total)
                send(half, 1, 0, 2, 0, "first", -1)
                send(half, 1, 0, 2, 0, "second", 1)
            elif c != 0:
                name = "first" if c == -1 else "second"
                arrived = receive(half, 1, 0, c, 0, name, c)
                zero = jnp.zeros_like(arrived)
                pieces = [arrived, zero] if name == "first" else [zero, arrived]
                put(half, c, 0, "all", total + jnp.concatenate(pieces, axis=1))
                send(half, 1, 0, c, 0, "all", c)
            else:
                for step in (1, -1):
                    total = total + receive(half, 1, 0, 0, 0, "all", step)
                put(half, 0, 0, "all", total)
                part[place.own, :, span(half, "all"), :] = total
    out = remote(sbuf.at[place.own, 1 - place.zh], rz, zs.at[2], zr.at[2], place.partner())
    out.start()
    out.wait_recv()
    dnormed = part[place.own, place.zh] + rz[...].astype(F32)
    scaled = dnormed * gain_cols
    dtrans_out[...] = trans_scale * (scaled - trans_ref[...] * pull)
    out.wait_send()
    for copy in sent:
        copy.wait_send()
    gather_x.drain()
    gather_lt.drain()
    table.drain()
    x_copy.wait()


def last_kernel(x, dtrans, kl, grad, grad_bias, kl_mean):
    rounded = dtrans[...].astype(BF16)
    for k in range(4):
        for zh in (0, 1):
            v = zh * 4 + k
            grad[v * FB : (v + 1) * FB, :] = lax.dot_general(
                x[k, zh], rounded, (((0,), (0,)), ((), ())), preferred_element_type=F32
            ).astype(BF16)

    @pl.when(pl.program_id(0) == 0)
    def _():
        grad_bias[...] = jnp.sum(dtrans[...], axis=0, keepdims=True)
        kl_mean[0] = jnp.sum(kl[...]) / ROWS


def per_device(hidden, final_hidden, row_pick, trans_weight, trans_bias, norm_gain, unembed):
    whole = pl.BlockSpec(memory_space=pltpu.VMEM)
    anywhere = pl.BlockSpec(memory_space=pl.ANY)
    dma = pltpu.SemaphoreType.DMA
    shape = jax.ShapeDtypeStruct
    block = pltpu.VMEM((16, 2, ROWS, FB), BF16)
    x_all, dtrans, kl = pl.pallas_call(
        kernel,
        name="lens",
        out_shape=(shape((16, 2, ROWS, FB), BF16), shape((ROWS, FB), F32), shape((1, ROWS), F32)),
        in_specs=[whole, whole, whole, anywhere, whole, whole, anywhere],
        out_specs=(anywhere, whole, whole),
        scratch_shapes=[
            block,
            pltpu.VMEM((16, 2, 2 * ROWS, FB), BF16),
            pltpu.VMEM((NS, POOL // NS, FB), BF16),
            pltpu.VMEM((D, FB), BF16),
            pltpu.VMEM((NS, SHARD, VOC), BF16),
            pltpu.VMEM((ROWS, FB), F32),
            pltpu.VMEM((2 * ROWS, VOC), F32),
            pltpu.VMEM((NV, 8, 128), F32),
            pltpu.VMEM((NV, 8, 128), F32),
            pltpu.VMEM((16, 2, ROWS, FB), F32),
            block,
            block,
            block,
            block,
            pltpu.VMEM((2, ROWS, FB), BF16),
            pltpu.VMEM((2, ROWS, FB), BF16),
            pltpu.VMEM((ROWS, FB), BF16),
            dma,
            dma,
            dma,
            dma((2, 4, CHUNKS)),
            dma((4, CHUNKS)),
            dma((NS, CHUNKS)),
            dma((NS,)),
            dma((NS,)),
            dma((3,)),
            dma((3,)),
        ]
        + [dma((N_MSG,))] * 6
        + [dma((NV,))] * 4,
        compiler_params=pltpu.CompilerParams(
            collective_id=0, has_side_effects=True, vmem_limit_bytes=VMEM_LIMIT
        ),
    )(row_pick, hidden[0], final_hidden, trans_weight[0], trans_bias, norm_gain, unembed)
    grad_weight, grad_bias, kl_mean = pl.pallas_call(
        last_kernel,
        name="weight_gradient",
        grid=(4,),
        out_shape=(shape((D, FB), BF16), shape((1, FB), F32), shape((1,), F32)),
        in_specs=[
            pl.BlockSpec((4, 2, ROWS, FB), lambda y: (y, 0, 0, 0)),
            pl.BlockSpec((ROWS, FB), lambda y: (0, 0)),
            pl.BlockSpec((1, ROWS), lambda y: (0, 0)),
        ],
        out_specs=(
            pl.BlockSpec((D // 4, FB), lambda y: (y, 0)),
            pl.BlockSpec((1, FB), lambda y: (0, 0)),
            pl.BlockSpec(memory_space=pltpu.SMEM),
        ),
    )(x_all, dtrans, kl)
    return grad_weight[None], grad_bias, kl_mean


def solution(mesh):
    placed = (
        P("section", None, "vocab"),
        P("section", "vocab"),
        P("section", None),
        P("section", None, "vocab"),
        P("section", "vocab"),
        P("vocab"),
        P("section", "vocab"),
    )
    return jax.shard_map(
        per_device,
        mesh=mesh,
        in_specs=placed,
        out_specs=(P("section", None, "vocab"), P("section", "vocab"), P("section")),
        check_vma=False,
    )
```

```python
import jax
import jax.numpy as jnp
from jax import lax
from jax.experimental import pallas as pl
from jax.experimental.pallas import tpu as pltpu
from jax.sharding import PartitionSpec as P

MESH = pl.DeviceIdType.MESH
F32, BF16 = jnp.float32, jnp.bfloat16
EPS = 1e-05
NV, NS = 32, 8
ROWS, POOL, D, VOC, FB = 128, 512, 8192, 512, 256
VMEM_LIMIT = 60 * 1024 * 1024
N_MSG = 40
CHUNKS = 2
SHARD = D // NS
PIECE = SHARD // CHUNKS


def vid(y, x, zh):
    return y * 8 + zh * 4 + x


def ring(a, c):
    return lax.rem(a + (c + 4), 4)


class Place:
    def __init__(self):
        self.v = lax.axis_index("vocab")
        self.s = lax.axis_index("section")
        self.x = lax.rem(self.v, 4)
        self.zh = lax.rem(self.v // 4, 2)
        self.y = self.v // 8
        self.own = self.y * 4 + self.x

    def to(self, v):
        return (self.s, v)

    def partner(self):
        return self.to(vid(self.y, self.x, 1 - self.zh))

    def along_z(self, step):
        z = lax.rem(self.zh * 4 + self.s // 2 + (step + 8), 8)
        return (lax.rem(z, 4) * 2 + lax.rem(self.s, 2), vid(self.y, self.x, z // 4))

    def touching(self):
        across = (self.s + 1 - 2 * lax.rem(self.s, 2), self.v)
        sides = [self.near(half, 1, step) for half in (0, 1) for step in (1, -1)]
        return sides + [self.along_z(1), self.along_z(-1), across]

    def near(self, half, stage, step):
        along_x = (half == 0) == (stage == 1)
        if along_x:
            return self.to(vid(self.y, ring(self.x, step), self.zh))
        return self.to(vid(ring(self.y, step), self.x, self.zh))

    def pair(self, half, c, d):
        if half == 0:
            return ring(self.y, d) * 4 + ring(self.x, c)
        return ring(self.y, c) * 4 + ring(self.x, d)


def remote(src, dst, send_sem, recv_sem, device):
    return pltpu.make_async_remote_copy(
        src_ref=src, dst_ref=dst, send_sem=send_sem, recv_sem=recv_sem, device_id=device, device_id_type=MESH
    )


def announce(place):
    barrier = pltpu.get_barrier_semaphore()
    for device in place.touching():
        pl.semaphore_signal(barrier, inc=1, device_id=device, device_id_type=MESH)


def await_touching(place):
    pl.semaphore_wait(pltpu.get_barrier_semaphore(), len(place.touching()))


def widen(place, known, turn):
    for side in (0, 1):
        pl.semaphore_signal(
            known.at[turn, side], inc=1, device_id=place.along_z(1 - 2 * side), device_id_type=MESH
        )
    for side in (0, 1):
        pl.semaphore_wait(known.at[turn, side], 1)


def send_stats(place, stats, send_sem, recv_sem):
    @pl.loop(1, NV)
    def _(k):
        remote(
            stats.at[place.v],
            stats.at[place.v],
            send_sem.at[k],
            recv_sem.at[place.v],
            place.to(lax.rem(place.v + k, NV)),
        ).start()


def wait_stats(place, stats, send_sem, recv_sem):
    @pl.loop(1, NV)
    def _(k):
        src = lax.rem(place.v + k, NV)
        copy = remote(stats.at[src], stats.at[src], send_sem.at[k], recv_sem.at[src], place.to(src))
        copy.wait_send()
        copy.wait_recv()


def to_lanes(columns):
    lane = lax.broadcasted_iota(jnp.int32, (ROWS, 128), 1)
    tile = jnp.zeros((ROWS, 128), F32)
    for k, column in enumerate(columns):
        tile = jnp.where(lane == k, column, tile)
    return tile.T[0:8, :]


def to_columns(tile):
    return jnp.concatenate([tile, jnp.zeros((120, 128), F32)], axis=0).T


class Gather:
    ORDER = (0, -1, 1, 2)

    def __init__(self, place, buf, send_sem, recv_sem):
        self.place, self.buf, self.ss, self.rs = place, buf, send_sem, recv_sem
        self.rows = buf.shape[2]
        self.sent = []
        self.ids = {}

    def span(self, half, part):
        h, q = self.rows // 2, self.rows // 4
        if part == "all":
            return pl.ds(half * h, h)
        return pl.ds(half * h + (0 if part == "first" else q), q)

    def key(self, *name):
        return self.ids.setdefault(name, len(self.ids))

    def move(self, name, pair, half, part, device):
        ref = self.buf.at[pair, :, self.span(half, part), :]
        k = self.key(*name)
        return remote(ref, ref, self.ss.at[k], self.rs.at[k], device)

    def send(self, half, stage, col, c, d, part, step):
        p = self.place
        copy = self.move((half, stage, col, part, step), p.pair(half, c, d), half, part, p.near(half, stage, step))
        copy.start()
        self.sent.append(copy)

    def wait(self, half, stage, col, c, d, part, step):
        p = self.place
        self.move((half, stage, col, part, step), p.pair(half, c, d), half, part, p.near(half, stage, -step)).wait_recv()

    def partner(self, zsend, zrecv):
        p = self.place
        mine = self.buf.at[p.own, p.zh]
        return (
            remote(mine, mine, zsend, zrecv, p.partner()),
            remote(self.buf.at[p.own, 1 - p.zh], self.buf.at[p.own, 1 - p.zh], zsend, zrecv, p.partner()),
        )

    def run(self, zsend, zrecv, hooks):
        def reach(point):
            if point in hooks:
                hooks[point]()

        out, back = self.partner(zsend, zrecv)
        out.start()
        reach("start")
        back.wait_recv()
        for half in (0, 1):
            for step in (1, -1):
                self.send(half, 1, 0, 0, 0, "all", step)
        for half in (0, 1):
            for step in (1, -1):
                self.send(half, 2, 0, 0, 0, "all", step)
        reach("sent")
        for step, part in ((1, "first"), (-1, "second")):
            for half in (0, 1):
                self.wait(half, 1, 0, -step, 0, "all", step)
                self.send(half, 1, 0, -step, 0, part, step)
                for turn in (1, -1):
                    self.send(half, 2, -step, -step, 0, "all", turn)
        for step, part in ((1, "first"), (-1, "second")):
            for half in (0, 1):
                self.wait(half, 2, 0, 0, -step, "all", step)
                self.send(half, 2, 0, 0, -step, part, step)
        for half in (0, 1):
            self.wait(half, 1, 0, 2, 0, "first", 1)
            self.wait(half, 1, 0, 2, 0, "second", -1)
            for turn in (1, -1):
                self.send(half, 2, 2, 2, 0, "all", turn)
        reach("turned")
        for c in (-1, 1, 2):
            for step, part in ((1, "first"), (-1, "second")):
                for half in (0, 1):
                    self.wait(half, 2, c, c, -step, "all", step)
                    self.send(half, 2, c, c, -step, part, step)
        for c in self.ORDER:
            for half in (0, 1):
                self.wait(half, 2, c, c, 2, "first", 1)
                self.wait(half, 2, c, c, 2, "second", -1)
        out.wait_send()

    def drain(self):
        for copy in self.sent:
            copy.wait_send()


class Table:
    def __init__(self, place, mine, buf, to_z, to_core, arrived, local):
        self.place, self.mine, self.buf = place, mine, buf
        self.to_z, self.to_core, self.arrived, self.local = to_z, to_core, arrived, local
        self.core = lax.rem(place.s, 2)
        self.zl = place.s // 2

    def piece(self, shard, part):
        return self.buf.at[shard, pl.ds(part * PIECE, PIECE), :]

    def along(self, i, part, sign, src=None):
        shard = 2 * i + self.core
        here = self.piece(shard, part) if src is None else src
        return remote(
            here,
            self.piece(shard, part),
            self.to_z.at[0 if sign > 0 else 1, i, part],
            self.arrived.at[shard, part],
            (self.place.s + 2 * sign, self.place.v),
        )

    def across(self, i, part, src=None):
        shard = 2 * i + self.core
        here = self.piece(shard, part) if src is None else src
        return remote(
            here,
            self.piece(shard, part),
            self.to_core.at[i, part],
            self.arrived.at[shard, part],
            (self.place.s + 1 - 2 * self.core, self.place.v),
        )

    def start(self):
        for part in range(CHUNKS):
            src = self.mine.at[pl.ds(part * PIECE, PIECE), :]

            @pl.when(self.zl < 3)
            def _():
                self.along(self.zl, part, 1, src).start()

            @pl.when(self.zl > 0)
            def _():
                self.along(self.zl, part, -1, src).start()

        for part in range(CHUNKS):
            self.across(self.zl, part, self.mine.at[pl.ds(part * PIECE, PIECE), :]).start()
        pltpu.make_async_copy(self.mine, self.buf.at[self.place.s], self.local).start()

    def wait(self, shard, part):
        ref = self.piece(shard, part)
        remote(ref, ref, self.to_core.at[0, part], self.arrived.at[shard, part], (self.place.s, self.place.v)).wait_recv()

    def relay(self, wave, part):
        for side in (-1, 1):
            i = self.zl + side * wave
            beyond = self.zl - side

            @pl.when((i >= 0) & (i <= 3))
            def _():
                self.wait(2 * i + self.core, part)

                @pl.when((beyond >= 0) & (beyond <= 3))
                def _():
                    self.along(i, part, -side).start()

                self.across(i, part).start()

    def drain(self):
        for part in range(CHUNKS):
            for i in range(4):

                @pl.when((self.zl < 3) & (self.zl >= i))
                def _():
                    self.along(i, part, 1).wait_send()

                @pl.when((self.zl > 0) & (self.zl <= i))
                def _():
                    self.along(i, part, -1).wait_send()

                self.across(i, part).wait_send()


class Finals:
    def __init__(self, place, mine, buf, to_z, to_core, arrived):
        self.place, self.mine, self.buf = place, mine, buf
        self.to_z, self.to_core, self.arrived = to_z, to_core, arrived
        self.core = lax.rem(place.s, 2)
        self.zl = place.s // 2

    def along(self, k):
        i = lax.rem(self.zl + k, 4)
        return remote(
            self.mine,
            self.buf.at[self.place.s],
            self.to_z.at[k],
            self.arrived.at[self.place.s],
            (2 * i + self.core, self.place.v),
        )

    def across(self, k):
        shard = 2 * lax.rem(self.zl + k, 4) + self.core
        here = self.mine if k == 0 else self.buf.at[shard]
        return remote(
            here,
            self.buf.at[shard],
            self.to_core.at[k],
            self.arrived.at[shard],
            (self.place.s + 1 - 2 * self.core, self.place.v),
        )

    def wait(self, shard):
        ref = self.buf.at[shard]
        remote(ref, ref, self.to_core.at[0], self.arrived.at[shard], (self.place.s, self.place.v)).wait_recv()

    def start(self):
        for k in (1, 2, 3):
            self.along(k).start()
        self.across(0).start()

    def forward(self):
        for k in (1, 2, 3):
            self.wait(2 * lax.rem(self.zl + k, 4) + self.core)
            self.across(k).start()

    def finish(self):
        for k in range(4):
            self.wait(2 * lax.rem(self.zl + k, 4) + 1 - self.core)

    def drain(self):
        for k in (1, 2, 3):
            self.along(k).wait_send()
        for k in range(4):
            self.across(k).wait_send()


def kernel(
    pick, hidden_hbm, final_hbm, w_hbm, bias, gain, u_mine, x_out, dtrans_out, kl_out,
    hidden, xbuf, xt, lt, fbuf, wbuf, u, trans_ref, acc, scale_stats, stats, part, sbuf, rq, rp, rm, r1p, r1m, rz,
    in_sem, x_sem, u_sem, uz, uc, ua, fz, fc, fa, known, zs, zr, ss1, rs1, ss2, rs2, ss, rs, sts1, str1, sts2, str2,
):
    place = Place()
    announce(place)
    table = Table(place, u_mine, u, uz, uc, ua, u_sem)
    pool = Finals(place, final_hbm, fbuf, fz, fc, fa)
    hidden_copy = pltpu.make_async_copy(hidden_hbm, hidden, in_sem.at[0])
    hidden_copy.start()
    final_copy = pltpu.make_async_copy(final_hbm, fbuf.at[place.s], in_sem.at[1])
    final_copy.start()
    w_copy = pltpu.make_async_copy(w_hbm, wbuf, in_sem.at[2])
    w_copy.start()
    chosen = jnp.broadcast_to(pick[...].astype(F32), (ROWS, ROWS)).T[:, 0:1].astype(jnp.int32)
    onehot = jnp.where(lax.broadcasted_iota(jnp.int32, (ROWS, POOL), 1) == chosen, 1.0, 0.0).astype(BF16)
    await_touching(place)
    table.start()
    hidden_copy.wait()
    inputs = jnp.dot(onehot, hidden[...], preferred_element_type=F32)
    xbuf[place.own, place.zh] = inputs.astype(BF16)
    for turn in range(3):
        widen(place, known, turn)
    gather_x = Gather(place, xbuf, ss1, rs1)
    gather_x.run(zs.at[0], zr.at[0], {"start": pool.start, "turned": lambda: table.relay(1, 0)})
    final_copy.wait()
    pool.forward()
    gain_cols = gain[...].astype(F32).reshape(1, FB)
    w_copy.wait()
    trans_ref[...] = xbuf[place.own, place.zh].astype(F32) + bias[...].astype(F32)

    @pl.loop(0, 16)
    def _(p):
        y, x = p // 4, lax.rem(p, 4)
        total = trans_ref[...]
        for zh in (0, 1):
            rows = pl.ds(pl.multiple_of(vid(y, x, zh) * FB, FB), FB)
            total = total + jnp.dot(xbuf[p, zh], wbuf[rows, :], preferred_element_type=F32)
        trans_ref[...] = total

    pool.finish()
    finals = jnp.dot(onehot, fbuf[...].reshape(POOL, FB), preferred_element_type=F32)
    trans = trans_ref[...]
    lt[place.own, place.zh, 0:ROWS] = (trans * gain_cols).astype(BF16)
    lt[place.own, place.zh, ROWS : 2 * ROWS] = (finals * gain_cols).astype(BF16)
    scale_stats[place.v] = to_lanes(
        [jnp.sum(trans * trans, axis=1, keepdims=True), jnp.sum(finals * finals, axis=1, keepdims=True)]
    )
    send_stats(place, scale_stats, sts1, str1)
    gather_lt = Gather(place, lt, ss2, rs2)
    gather_lt.run(
        zs.at[1], zr.at[1], {"sent": lambda: table.relay(1, 1), "turned": lambda: table.relay(2, 0)}
    )
    table.relay(2, 1)
    acc[...] = jnp.zeros_like(acc)

    def absorb(shard, first, count):
        total = acc[...]
        for k in range(first, first + count):
            total = total + jnp.dot(
                lt[(shard // 2) * 4 + k, lax.rem(shard, 2)],
                u[shard, k * FB : (k + 1) * FB, :],
                preferred_element_type=F32,
            )
        acc[...] = total

    pltpu.make_async_copy(u_mine, u.at[place.s], u_sem).wait()
    absorb(place.s, 0, 4)
    other = place.s + 1 - 2 * table.core
    for piece in range(CHUNKS):
        table.wait(other, piece)
    absorb(other, 0, 4)
    for wave in (1, 2, 3):
        if wave == 3:

            @pl.loop(0, 16)
            def _(p):
                for zh in (0, 1):
                    xt[p, zh] = xbuf[p, zh].astype(F32).T.astype(BF16)

            x_copy = pltpu.make_async_copy(xt, x_out, x_sem)
            x_copy.start()
        for piece in range(CHUNKS):
            if wave == 3:
                table.relay(3, piece)
            for side in (-1, 1):
                i = table.zl + side * wave

                @pl.when((i >= 0) & (i <= 3))
                def _():
                    per = 4 // CHUNKS
                    absorb(2 * i + table.core, piece * per, per)
                    table.wait(2 * i + 1 - table.core, piece)
                    absorb(2 * i + 1 - table.core, piece * per, per)

    wait_stats(place, scale_stats, sts1, str1)
    scale = lax.rsqrt(jnp.sum(scale_stats[...], axis=0) / D + EPS)


    columns = to_columns(scale)
    trans_scale, final_scale = columns[:, 0:1], columns[:, 1:2]
    logits = acc[0:ROWS] * trans_scale
    target = acc[ROWS : 2 * ROWS] * final_scale

    def totals(values):
        highest = jnp.max(values, axis=1, keepdims=True)
        shifted = values - highest
        weights = jnp.exp(shifted)
        return highest, shifted, weights, jnp.sum(weights, axis=1, keepdims=True)

    l_max, l_shift, l_exp, l_sum = totals(logits)
    t_max, t_shift, t_exp, t_sum = totals(target)
    stats[place.v] = to_lanes(
        [
            l_max,
            l_sum,
            jnp.sum(l_exp * l_shift, axis=1, keepdims=True),
            t_max,
            t_sum,
            jnp.sum(t_exp * t_shift, axis=1, keepdims=True),
            jnp.sum(t_exp * l_shift, axis=1, keepdims=True),
        ]
    )
    send_stats(place, stats, sts2, str2)
    wait_stats(place, stats, sts2, str2)
    lm, ls, la, tm, ts, ta, tb = (stats[:, k, :] for k in range(7))

    def over(values):
        return jnp.sum(values, axis=0, keepdims=True)

    l_top = jnp.max(lm, axis=0, keepdims=True)
    t_top = jnp.max(tm, axis=0, keepdims=True)
    lw, tw = jnp.exp(lm - l_top), jnp.exp(tm - t_top)
    l_total, t_total = over(lw * ls), over(tw * ts)
    mean_l = over(lw * (la + ls * (lm - l_top))) / l_total
    mean_t = over(tw * (ta + ts * (tm - t_top))) / t_total
    mean_tl = over(tw * (tb + ts * (lm - l_top))) / t_total
    kl_rows = mean_t - mean_tl - jnp.log(t_total) + jnp.log(l_total)
    kl_out[...] = kl_rows
    l_norm = l_top + jnp.log(l_total)
    t_norm = t_top + jnp.log(t_total)
    pull = scale[0:1, :] * (mean_l - mean_tl) / D
    columns = to_columns(jnp.concatenate([l_norm, t_norm, pull, jnp.zeros((5, 128), F32)], axis=0))
    l_norm, t_norm, pull = columns[:, 0:1], columns[:, 1:2], columns[:, 2:3]
    dlogits = (jnp.exp(logits - l_norm) - jnp.exp(target - t_norm)).astype(BF16)

    ids = {}
    sent = []
    half_rows, quarter = ROWS // 2, ROWS // 4

    def span(half, name):
        if name == "all":
            return pl.ds(half * half_rows, half_rows)
        return pl.ds(half * half_rows + (0 if name == "first" else quarter), quarter)

    def product(pair):
        y, x = pair // 4, lax.rem(pair, 4)
        for zh in (0, 1):
            rows = pl.ds(pl.multiple_of(x * FB, FB), FB)
            part[pair, zh] = lax.dot_general(
                dlogits, u[2 * y + zh, rows, :], (((1,), (1,)), ((), ())), preferred_element_type=F32
            )

    def move(name, src, dst, device):
        k = ids.setdefault(name, len(ids))
        return remote(src, dst, ss.at[k], rs.at[k], device)

    def landing(stage, name, step, pair, half):
        rows = span(half, name)
        if name != "all":
            return rq.at[pair, :, rows, :]
        if stage == 2:
            return (rp if step == 1 else rm).at[pair, :, rows, :]
        return (r1p if step == 1 else r1m).at[:, rows, :]

    def send(half, stage, col, c, d, name, step):
        pair = place.pair(half, c, d)
        copy = move(
            (half, stage, col, name, step),
            sbuf.at[pair, :, span(half, name), :],
            landing(stage, name, step, pair, half),
            place.near(half, stage, step),
        )
        copy.start()
        sent.append(copy)

    def receive(half, stage, col, c, d, name, step):
        pair = place.pair(half, c, d)
        ref = landing(stage, name, step, pair, half)
        move((half, stage, col, name, step), ref, ref, place.near(half, stage, -step)).wait_recv()
        return ref[...].astype(F32)

    def put(half, c, d, name, value):
        sbuf[place.pair(half, c, d), :, span(half, name), :] = value.astype(BF16)

    def mine(half, c, d, name):
        return part[place.pair(half, c, d), :, span(half, name), :]

    first = [(2, 2)] + [(2, k) for k in (-1, 1, 0)] + [(k, 2) for k in (-1, 1, 0)]
    later = [(-1, -1), (-1, 1), (1, -1), (1, 1), (0, -1), (0, 1), (-1, 0), (1, 0), (0, 0)]
    for dx, dy in first:
        product(place.pair(0, dx, dy))
        for half in (0, 1):
            c, d = (dx, dy) if half == 0 else (dy, dx)
            if d == 2:
                put(half, c, 2, "all", mine(half, c, 2, "all"))
                send(half, 2, c, c, 2, "first", -1)
                send(half, 2, c, c, 2, "second", 1)
    for dx, dy in later:
        product(place.pair(0, dx, dy))
    order = (2, -1, 1, 0)
    for c in order:
        for half in (0, 1):
            for step, name in ((-1, "first"), (1, "second")):
                arrived = receive(half, 2, c, c, step, name, step)
                put(half, c, step, "all", mine(half, c, step, "all"))
                put(half, c, step, name, mine(half, c, step, name) + arrived)
                send(half, 2, c, c, step, "all", step)
    own_sum = [None, None]
    for c in order:
        for half in (0, 1):
            total = mine(half, c, 0, "all")
            for step in (1, -1):
                total = total + receive(half, 2, c, c, 0, "all", step)
            if c == 2:
                put(half, 2, 0, "all", total)
                send(half, 1, 0, 2, 0, "first", -1)
                send(half, 1, 0, 2, 0, "second", 1)
            elif c != 0:
                name = "first" if c == -1 else "second"
                arrived = receive(half, 1, 0, c, 0, name, c)
                zero = jnp.zeros_like(arrived)
                pieces = [arrived, zero] if name == "first" else [zero, arrived]
                put(half, c, 0, "all", total + jnp.concatenate(pieces, axis=1))
                send(half, 1, 0, c, 0, "all", c)
            else:
                for step in (1, -1):
                    total = total + receive(half, 1, 0, 0, 0, "all", step)
                put(half, 0, 0, "all", total)
                part[place.own, :, span(half, "all"), :] = total
    out = remote(sbuf.at[place.own, 1 - place.zh], rz, zs.at[2], zr.at[2], place.partner())
    out.start()
    out.wait_recv()
    dnormed = part[place.own, place.zh] + rz[...].astype(F32)
    scaled = dnormed * gain_cols
    dtrans_out[...] = trans_scale * (scaled - trans_ref[...] * pull)
    out.wait_send()
    for copy in sent:
        copy.wait_send()
    gather_x.drain()
    gather_lt.drain()
    table.drain()
    pool.drain()
    x_copy.wait()


def last_kernel(x, dtrans, kl, grad, grad_bias, kl_mean):
    rounded = dtrans[...].astype(BF16)
    for k in range(4):
        for zh in (0, 1):
            v = zh * 4 + k
            grad[v * FB : (v + 1) * FB, :] = lax.dot_general(
                x[k, zh], rounded, (((1,), (0,)), ((), ())), preferred_element_type=F32
            ).astype(BF16)

    @pl.when(pl.program_id(0) == 0)
    def _():
        grad_bias[...] = jnp.sum(dtrans[...], axis=0, keepdims=True)
        kl_mean[0] = jnp.sum(kl[...]) / ROWS


def per_device(hidden, final_hidden, row_pick, trans_weight, trans_bias, norm_gain, unembed):
    whole = pl.BlockSpec(memory_space=pltpu.VMEM)
    anywhere = pl.BlockSpec(memory_space=pl.ANY)
    dma = pltpu.SemaphoreType.DMA
    shape = jax.ShapeDtypeStruct
    block = pltpu.VMEM((16, 2, ROWS, FB), BF16)
    x_all, dtrans, kl = pl.pallas_call(
        kernel,
        name="lens",
        out_shape=(shape((16, 2, FB, ROWS), BF16), shape((ROWS, FB), F32), shape((1, ROWS), F32)),
        in_specs=[whole, anywhere, anywhere, anywhere, whole, whole, anywhere],
        out_specs=(anywhere, whole, whole),
        scratch_shapes=[
            pltpu.VMEM((POOL, FB), BF16),
            block,
            pltpu.VMEM((16, 2, FB, ROWS), BF16),
            pltpu.VMEM((16, 2, 2 * ROWS, FB), BF16),
            pltpu.VMEM((NS, POOL // NS, FB), BF16),
            pltpu.VMEM((D, FB), BF16),
            pltpu.VMEM((NS, SHARD, VOC), BF16),
            pltpu.VMEM((ROWS, FB), F32),
            pltpu.VMEM((2 * ROWS, VOC), F32),
            pltpu.VMEM((NV, 8, 128), F32),
            pltpu.VMEM((NV, 8, 128), F32),
            pltpu.VMEM((16, 2, ROWS, FB), F32),
            block,
            block,
            block,
            block,
            pltpu.VMEM((2, ROWS, FB), BF16),
            pltpu.VMEM((2, ROWS, FB), BF16),
            pltpu.VMEM((ROWS, FB), BF16),
            dma((3,)),
            dma,
            dma,
            dma((2, 4, CHUNKS)),
            dma((4, CHUNKS)),
            dma((NS, CHUNKS)),
            dma((4,)),
            dma((4,)),
            dma((NS,)),
            pltpu.SemaphoreType.REGULAR((3, 2)),
            dma((3,)),
            dma((3,)),
        ]
        + [dma((N_MSG,))] * 6
        + [dma((NV,))] * 4,
        compiler_params=pltpu.CompilerParams(
            collective_id=0, has_side_effects=True, vmem_limit_bytes=VMEM_LIMIT
        ),
    )(row_pick, hidden[0], final_hidden, trans_weight[0], trans_bias, norm_gain, unembed)
    grad_weight, grad_bias, kl_mean = pl.pallas_call(
        last_kernel,
        name="weight_gradient",
        grid=(4,),
        out_shape=(shape((D, FB), BF16), shape((1, FB), F32), shape((1,), F32)),
        in_specs=[
            pl.BlockSpec((4, 2, FB, ROWS), lambda y: (y, 0, 0, 0)),
            pl.BlockSpec((ROWS, FB), lambda y: (0, 0)),
            pl.BlockSpec((1, ROWS), lambda y: (0, 0)),
        ],
        out_specs=(
            pl.BlockSpec((D // 4, FB), lambda y: (y, 0)),
            pl.BlockSpec((1, FB), lambda y: (0, 0)),
            pl.BlockSpec(memory_space=pltpu.SMEM),
        ),
    )(x_all, dtrans, kl)
    return grad_weight[None], grad_bias, kl_mean


def solution(mesh):
    placed = (
        P("section", None, "vocab"),
        P("section", "vocab"),
        P("section", None),
        P("section", None, "vocab"),
        P("section", "vocab"),
        P("vocab"),
        P("section", "vocab"),
    )
    return jax.shard_map(
        per_device,
        mesh=mesh,
        in_specs=placed,
        out_specs=(P("section", None, "vocab"), P("section", "vocab"), P("section")),
        check_vma=False,
    )
```

```python
import jax
import jax.numpy as jnp
from jax import lax
from jax.experimental import pallas as pl
from jax.experimental.pallas import tpu as pltpu
from jax.sharding import PartitionSpec as P

MESH = pl.DeviceIdType.MESH
F32, BF16 = jnp.float32, jnp.bfloat16
EPS = 1e-05
NV, NS = 32, 8
ROWS, POOL, D, VOC, FB = 128, 512, 8192, 512, 256
VMEM_LIMIT = 60 * 1024 * 1024
N_MSG = 30
STEPS = (1, -1, 2)
CHUNKS = 4
SHARD = D // NS
PIECE = SHARD // CHUNKS


def vid(y, x, zh):
    return y * 8 + zh * 4 + x


def ring(a, c):
    return lax.rem(a + (c + 4), 4)


class Place:
    def __init__(self):
        self.v = lax.axis_index("vocab")
        self.s = lax.axis_index("section")
        self.x = lax.rem(self.v, 4)
        self.zh = lax.rem(self.v // 4, 2)
        self.y = self.v // 8
        self.own = self.y * 4 + self.x

    def to(self, v):
        return (self.s, v)

    def partner(self):
        return self.to(vid(self.y, self.x, 1 - self.zh))

    def along_z(self, step):
        z = lax.rem(self.zh * 4 + self.s // 2 + (step + 8), 8)
        return (lax.rem(z, 4) * 2 + lax.rem(self.s, 2), vid(self.y, self.x, z // 4))

    def touching(self):
        across = (self.s + 1 - 2 * lax.rem(self.s, 2), self.v)
        sides = [self.near(half, 1, step) for half in (0, 1) for step in (1, -1)]
        return sides + [self.along_z(1), self.along_z(-1), across]

    def near(self, half, stage, step):
        along_x = (half == 0) == (stage == 1)
        if along_x:
            return self.to(vid(self.y, ring(self.x, step), self.zh))
        return self.to(vid(ring(self.y, step), self.x, self.zh))

    def pair(self, half, c, d):
        if half == 0:
            return ring(self.y, d) * 4 + ring(self.x, c)
        return ring(self.y, c) * 4 + ring(self.x, d)


def remote(src, dst, send_sem, recv_sem, device):
    return pltpu.make_async_remote_copy(
        src_ref=src, dst_ref=dst, send_sem=send_sem, recv_sem=recv_sem, device_id=device, device_id_type=MESH
    )


def announce(place):
    barrier = pltpu.get_barrier_semaphore()
    for device in place.touching():
        pl.semaphore_signal(barrier, inc=1, device_id=device, device_id_type=MESH)


def await_touching(place):
    pl.semaphore_wait(pltpu.get_barrier_semaphore(), len(place.touching()))


def widen_plane(place, known):
    for half in (0, 1):
        for side in (0, 1):
            pl.semaphore_signal(
                known.at[3 + half, side],
                inc=1,
                device_id=place.near(half, 1, 1 - 2 * side),
                device_id_type=MESH,
            )
    for half in (0, 1):
        for side in (0, 1):
            pl.semaphore_wait(known.at[3 + half, side], 1)


def widen(place, known, turn):
    for side in (0, 1):
        pl.semaphore_signal(
            known.at[turn, side], inc=1, device_id=place.along_z(1 - 2 * side), device_id_type=MESH
        )
    for side in (0, 1):
        pl.semaphore_wait(known.at[turn, side], 1)


def send_stats(place, stats, send_sem, recv_sem):
    @pl.loop(1, NV)
    def _(k):
        remote(
            stats.at[place.v],
            stats.at[place.v],
            send_sem.at[k],
            recv_sem.at[place.v],
            place.to(lax.rem(place.v + k, NV)),
        ).start()


def wait_stats(place, stats, send_sem, recv_sem):
    @pl.loop(1, NV)
    def _(k):
        src = lax.rem(place.v + k, NV)
        copy = remote(stats.at[src], stats.at[src], send_sem.at[k], recv_sem.at[src], place.to(src))
        copy.wait_send()
        copy.wait_recv()


def to_lanes(columns):
    lane = lax.broadcasted_iota(jnp.int32, (ROWS, 128), 1)
    tile = jnp.zeros((ROWS, 128), F32)
    for k, column in enumerate(columns):
        tile = jnp.where(lane == k, column, tile)
    return tile.T[0:8, :]


def to_columns(tile):
    return jnp.concatenate([tile, jnp.zeros((120, 128), F32)], axis=0).T


class Plane:
    def __init__(self, place, buf, level, base, send_sem, recv_sem):
        self.place, self.buf, self.level, self.base = place, buf, level, base
        self.ss, self.rs = send_sem, recv_sem
        self.sent = []
        self.ids = {}

    def move(self, name, pair, half, device):
        rows = pl.ds(self.base + half * (ROWS // 2), ROWS // 2)
        ref = self.buf.at[pair, self.level, rows, :]
        k = self.ids.setdefault(name, len(self.ids))
        return remote(ref, ref, self.ss.at[k], self.rs.at[k], device)

    def first(self, half, c):
        p = self.place
        self.sent.append(self.move((half, c), p.own, half, p.near(half, 1, c)))
        self.sent[-1].start()

    def second(self, half, c, d):
        p = self.place
        self.sent.append(self.move((half, c, d), p.pair(half, -c, 0), half, p.near(half, 2, d)))
        self.sent[-1].start()

    def steps(self):
        p = self.place
        for c in STEPS:
            for half in (0, 1):
                self.first(half, c)
        for d in STEPS:
            for half in (0, 1):
                self.second(half, 0, d)
        yield
        for c in STEPS:
            for half in (0, 1):
                self.move((half, c), p.pair(half, -c, 0), half, p.near(half, 1, -c)).wait_recv()
                for d in STEPS:
                    self.second(half, c, d)
            yield
        for c in (0,) + STEPS:
            for half in (0, 1):
                for d in STEPS:
                    self.move((half, c, d), p.pair(half, -c, -d), half, p.near(half, 2, -d)).wait_recv()
        yield

    def drain(self):
        for copy in self.sent:
            copy.wait_send()


class Scatter:
    def __init__(self, place, level, product, refs, send_sem, recv_sem):
        self.place, self.level, self.product = place, level, product
        self.part, self.sbuf, self.arrive, self.last = refs
        self.ss, self.rs = send_sem, recv_sem
        self.sent = []
        self.ids = {}

    def rows(self, half):
        return pl.ds(half * (ROWS // 2), ROWS // 2)

    def landing(self, name, pair):
        if len(name) == 3:
            return self.arrive[STEPS.index(name[2])].at[pair, self.level, self.rows(name[0]), :]
        return self.last[STEPS.index(name[1])].at[self.level, self.rows(name[0]), :]

    def move(self, name, src, dst, device):
        k = self.ids.setdefault(name, len(self.ids))
        return remote(src, dst, self.ss.at[k], self.rs.at[k], device)

    def send(self, name, pair, device, value):
        half = name[0]
        self.sbuf[pair, self.level, self.rows(half), :] = value.astype(BF16)
        src = self.sbuf.at[pair, self.level, self.rows(half), :]
        self.sent.append(self.move(name, src, self.landing(name, pair), device))
        self.sent[-1].start()

    def receive(self, name, pair, device):
        ref = self.landing(name, pair)
        self.move(name, ref, ref, device).wait_recv()
        return ref[...].astype(F32)

    def mine(self, half, c, d):
        return self.part[self.place.pair(half, c, d), self.level, self.rows(half), :]

    def open(self):
        p = self.place
        order = [(a, b) for a in (2, 1, -1) for b in (2, 1, -1)]
        order += [(a, 0) for a in (2, 1, -1)] + [(0, b) for b in (2, 1, -1)] + [(0, 0)]
        for dx, dy in order:
            pair = p.pair(0, dx, dy)
            self.product(pair, self.level)
            for half in (0, 1):
                c, d = (dx, dy) if half == 0 else (dy, dx)
                if d != 0:
                    self.send((half, c, d), pair, p.near(half, 2, d), self.mine(half, c, d))

    def column(self, half, c):
        p = self.place
        total = self.mine(half, c, 0)
        for d in STEPS:
            total = total + self.receive((half, c, d), p.pair(half, c, 0), p.near(half, 2, -d))
        return total

    def turn(self):
        p = self.place
        for c in (2, 1, -1):
            for half in (0, 1):
                self.send((half, c), p.pair(half, c, 0), p.near(half, 1, c), self.column(half, c))

    def close(self):
        p = self.place
        for half in (0, 1):
            total = self.column(half, 0)
            for c in STEPS:
                total = total + self.receive((half, c), p.own, p.near(half, 1, -c))
            self.sbuf[p.own, self.level, self.rows(half), :] = total.astype(BF16)
            self.part[p.own, self.level, self.rows(half), :] = total


class Table:
    def __init__(self, place, mine, buf, to_z, to_core, arrived, local):
        self.place, self.mine, self.buf = place, mine, buf
        self.to_z, self.to_core, self.arrived, self.local = to_z, to_core, arrived, local
        self.core = lax.rem(place.s, 2)
        self.zl = place.s // 2

    def piece(self, shard, part):
        return self.buf.at[shard, pl.ds(part * PIECE, PIECE), :]

    def along(self, i, part, sign, src=None):
        shard = 2 * i + self.core
        here = self.piece(shard, part) if src is None else src
        return remote(
            here,
            self.piece(shard, part),
            self.to_z.at[0 if sign > 0 else 1, i, part],
            self.arrived.at[shard, part],
            (self.place.s + 2 * sign, self.place.v),
        )

    def across(self, i, part, src=None):
        shard = 2 * i + self.core
        here = self.piece(shard, part) if src is None else src
        return remote(
            here,
            self.piece(shard, part),
            self.to_core.at[i, part],
            self.arrived.at[shard, part],
            (self.place.s + 1 - 2 * self.core, self.place.v),
        )

    def start(self, parts):
        for part in parts:
            src = self.mine.at[pl.ds(part * PIECE, PIECE), :]

            @pl.when(self.zl < 3)
            def _():
                self.along(self.zl, part, 1, src).start()

            @pl.when(self.zl > 0)
            def _():
                self.along(self.zl, part, -1, src).start()

            self.across(self.zl, part, src).start()

    def wait(self, shard, part):
        ref = self.piece(shard, part)
        remote(ref, ref, self.to_core.at[0, part], self.arrived.at[shard, part], (self.place.s, self.place.v)).wait_recv()

    def relay(self, wave, part):
        for side in (-1, 1):
            i = self.zl + side * wave
            beyond = self.zl - side

            @pl.when((i >= 0) & (i <= 3))
            def _():
                self.wait(2 * i + self.core, part)

                @pl.when((beyond >= 0) & (beyond <= 3))
                def _():
                    self.along(i, part, -side).start()

                self.across(i, part).start()

    def drain(self):
        for part in range(CHUNKS):
            for i in range(4):

                @pl.when((self.zl < 3) & (self.zl >= i))
                def _():
                    self.along(i, part, 1).wait_send()

                @pl.when((self.zl > 0) & (self.zl <= i))
                def _():
                    self.along(i, part, -1).wait_send()

                self.across(i, part).wait_send()


class Finals:
    def __init__(self, place, mine, buf, to_z, to_core, arrived):
        self.place, self.mine, self.buf = place, mine, buf
        self.to_z, self.to_core, self.arrived = to_z, to_core, arrived
        self.core = lax.rem(place.s, 2)
        self.zl = place.s // 2

    def along(self, k):
        i = lax.rem(self.zl + k, 4)
        return remote(
            self.mine,
            self.buf.at[self.place.s],
            self.to_z.at[k],
            self.arrived.at[self.place.s],
            (2 * i + self.core, self.place.v),
        )

    def across(self, k):
        shard = 2 * lax.rem(self.zl + k, 4) + self.core
        here = self.mine if k == 0 else self.buf.at[shard]
        return remote(
            here,
            self.buf.at[shard],
            self.to_core.at[k],
            self.arrived.at[shard],
            (self.place.s + 1 - 2 * self.core, self.place.v),
        )

    def wait(self, shard):
        ref = self.buf.at[shard]
        remote(ref, ref, self.to_core.at[0], self.arrived.at[shard], (self.place.s, self.place.v)).wait_recv()

    def start(self):
        for k in (1, 2, 3):
            self.along(k).start()
        self.across(0).start()

    def forward(self):
        for k in (1, 2, 3):
            self.wait(2 * lax.rem(self.zl + k, 4) + self.core)
            self.across(k).start()

    def finish(self):
        for k in range(4):
            self.wait(2 * lax.rem(self.zl + k, 4) + 1 - self.core)

    def drain(self):
        for k in (1, 2, 3):
            self.along(k).wait_send()
        for k in range(4):
            self.across(k).wait_send()


def kernel(
    pick, hidden_hbm, final_hbm, w_hbm, bias, gain, u_mine, x_out, dtrans_out, kl_out,
    hidden, xbuf, xt, lt, fbuf, wbuf, u, trans_ref, acc, scale_stats, stats, part, sbuf, rq, rp, rm, r1p, r1m, r1q, rz,
    in_sem, x_sem, u_sem, uz, uc, ua, fz, fc, fa, known, zs, zr, pss, prs, ss, rs, sts1, str1, sts2, str2,
):
    place = Place()
    announce(place)
    table = Table(place, u_mine, u, uz, uc, ua, u_sem)
    pool = Finals(place, final_hbm, fbuf, fz, fc, fa)
    hidden_copy = pltpu.make_async_copy(hidden_hbm, hidden, in_sem.at[0])
    hidden_copy.start()
    final_copy = pltpu.make_async_copy(final_hbm, fbuf.at[place.s], in_sem.at[1])
    final_copy.start()
    w_copy = pltpu.make_async_copy(w_hbm, wbuf, in_sem.at[2])
    w_copy.start()
    chosen = jnp.broadcast_to(pick[...].astype(F32), (ROWS, ROWS)).T[:, 0:1].astype(jnp.int32)
    onehot = jnp.where(lax.broadcasted_iota(jnp.int32, (ROWS, POOL), 1) == chosen, 1.0, 0.0).astype(BF16)
    gain_cols = gain[...].astype(F32).reshape(1, FB)

    planes = []

    def plane(buf, level, base):
        k = len(planes)
        planes.append(Plane(place, buf, level, base, pss.at[k], prs.at[k]))
        return planes[-1].steps()

    def go(steps, count=1):
        for _ in range(count):
            next(steps)

    def crossing(buf, base, k, level):
        ref = buf.at[place.own, level, pl.ds(base, ROWS), :]
        return remote(ref, ref, zs.at[k], zr.at[k], place.partner())

    near_x, far_x = plane(xbuf, place.zh, 0), plane(xbuf, 1 - place.zh, 0)
    near_t, far_t = plane(lt, place.zh, ROWS), plane(lt, 1 - place.zh, ROWS)
    near_l, far_l = plane(lt, place.zh, 0), plane(lt, 1 - place.zh, 0)

    def multiply(level):
        @pl.loop(0, 4)
        def _(y):
            total = trans_ref[...]
            for x in range(4):
                rows = pl.ds(pl.multiple_of(vid(y, x, level) * FB, FB), FB)
                total = total + jnp.dot(xbuf[y * 4 + x, level], wbuf[rows, :], preferred_element_type=F32)
            trans_ref[...] = total

    await_touching(place)
    table.start((0, 1))
    hidden_copy.wait()
    inputs = jnp.dot(onehot, hidden[...], preferred_element_type=F32)
    xbuf[place.own, place.zh] = inputs.astype(BF16)
    trans_ref[...] = inputs + bias[...].astype(F32)
    widen_plane(place, known)
    go(near_x)
    widen(place, known, 0)
    go(near_x, 2)
    widen(place, known, 1)
    pool.start()
    go(near_x)
    widen(place, known, 2)
    cross_x = crossing(xbuf, 0, 0, place.zh)
    cross_x.start()
    table.start((2, 3))
    u_copy = pltpu.make_async_copy(u_mine, u.at[place.s], u_sem)
    u_copy.start()
    go(near_x)
    crossing(xbuf, 0, 0, 1 - place.zh).wait_recv()
    go(far_x)
    final_copy.wait()
    pool.forward()
    go(far_x, 3)
    table.relay(1, 0)
    pool.finish()
    finals = jnp.dot(onehot, fbuf[...].reshape(POOL, FB), preferred_element_type=F32)
    lt[place.own, place.zh, ROWS : 2 * ROWS] = (finals * gain_cols).astype(BF16)
    cross_t = crossing(lt, ROWS, 1, place.zh)
    cross_t.start()
    go(near_t)
    w_copy.wait()
    multiply(place.zh)
    table.relay(1, 1)
    go(near_t, 3)
    go(far_x)
    multiply(1 - place.zh)
    trans = trans_ref[...]
    lt[place.own, place.zh, 0:ROWS] = (trans * gain_cols).astype(BF16)
    cross_l = crossing(lt, 0, 2, place.zh)
    cross_l.start()
    go(near_l)
    scale_stats[place.v] = to_lanes(
        [jnp.sum(trans * trans, axis=1, keepdims=True), jnp.sum(finals * finals, axis=1, keepdims=True)]
    )
    send_stats(place, scale_stats, sts1, str1)
    table.relay(1, 2)
    go(near_l, 3)
    crossing(lt, ROWS, 1, 1 - place.zh).wait_recv()
    go(far_t)
    table.relay(1, 3)
    go(far_t, 3)
    crossing(lt, 0, 2, 1 - place.zh).wait_recv()
    go(far_l)
    table.relay(2, 0)
    go(far_l, 3)
    go(near_t)
    go(near_l)
    table.relay(2, 1)
    go(far_t)
    go(far_l)
    table.relay(2, 2)
    acc[...] = jnp.zeros_like(acc)

    def absorb(shard, first, count):
        total = acc[...]
        for k in range(first, first + count):
            total = total + jnp.dot(
                lt[(shard // 2) * 4 + k, lax.rem(shard, 2)],
                u[shard, k * FB : (k + 1) * FB, :],
                preferred_element_type=F32,
            )
        acc[...] = total

    def each_side(wave, then):
        for side in (-1, 1):
            i = table.zl + side * wave

            @pl.when((i >= 0) & (i <= 3))
            def _():
                then(2 * i + table.core, 2 * i + 1 - table.core)

    def absorb_pair(own, other):
        absorb(own, 0, 4)
        for piece in range(CHUNKS):
            table.wait(other, piece)
        absorb(other, 0, 4)

    u_copy.wait()
    absorb_pair(place.s, place.s + 1 - 2 * table.core)
    each_side(1, absorb_pair)
    table.relay(2, 3)
    each_side(2, absorb_pair)

    @pl.loop(0, 16)
    def _(p):
        for zh in (0, 1):
            xt[p, zh] = xbuf[p, zh].astype(F32).T.astype(BF16)

    x_copy = pltpu.make_async_copy(xt, x_out, x_sem)
    x_copy.start()
    for piece in range(CHUNKS):
        table.relay(3, piece)

        def absorb_piece(own, other):
            absorb(own, piece, 1)
            table.wait(other, piece)
            absorb(other, piece, 1)

        each_side(3, absorb_piece)
    wait_stats(place, scale_stats, sts1, str1)
    scale = lax.rsqrt(jnp.sum(scale_stats[...], axis=0) / D + EPS)


    columns = to_columns(scale)
    trans_scale, final_scale = columns[:, 0:1], columns[:, 1:2]
    logits = acc[0:ROWS] * trans_scale
    target = acc[ROWS : 2 * ROWS] * final_scale

    def totals(values):
        highest = jnp.max(values, axis=1, keepdims=True)
        shifted = values - highest
        weights = jnp.exp(shifted)
        return highest, shifted, weights, jnp.sum(weights, axis=1, keepdims=True)

    l_max, l_shift, l_exp, l_sum = totals(logits)
    t_max, t_shift, t_exp, t_sum = totals(target)
    stats[place.v] = to_lanes(
        [
            l_max,
            l_sum,
            jnp.sum(l_exp * l_shift, axis=1, keepdims=True),
            t_max,
            t_sum,
            jnp.sum(t_exp * t_shift, axis=1, keepdims=True),
            jnp.sum(t_exp * l_shift, axis=1, keepdims=True),
        ]
    )
    send_stats(place, stats, sts2, str2)
    wait_stats(place, stats, sts2, str2)
    lm, ls, la, tm, ts, ta, tb = (stats[:, k, :] for k in range(7))

    def over(values):
        return jnp.sum(values, axis=0, keepdims=True)

    l_top = jnp.max(lm, axis=0, keepdims=True)
    t_top = jnp.max(tm, axis=0, keepdims=True)
    lw, tw = jnp.exp(lm - l_top), jnp.exp(tm - t_top)
    l_total, t_total = over(lw * ls), over(tw * ts)
    mean_l = over(lw * (la + ls * (lm - l_top))) / l_total
    mean_t = over(tw * (ta + ts * (tm - t_top))) / t_total
    mean_tl = over(tw * (tb + ts * (lm - l_top))) / t_total
    kl_rows = mean_t - mean_tl - jnp.log(t_total) + jnp.log(l_total)
    kl_out[...] = kl_rows
    l_norm = l_top + jnp.log(l_total)
    t_norm = t_top + jnp.log(t_total)
    pull = scale[0:1, :] * (mean_l - mean_tl) / D
    columns = to_columns(jnp.concatenate([l_norm, t_norm, pull, jnp.zeros((5, 128), F32)], axis=0))
    l_norm, t_norm, pull = columns[:, 0:1], columns[:, 1:2], columns[:, 2:3]
    dlogits = (jnp.exp(logits - l_norm) - jnp.exp(target - t_norm)).astype(BF16)

    def product(pair, level):
        y, x = pair // 4, lax.rem(pair, 4)
        rows = pl.ds(pl.multiple_of(x * FB, FB), FB)
        part[pair, level] = lax.dot_general(
            dlogits, u[2 * y + level, rows, :], (((1,), (1,)), ((), ())), preferred_element_type=F32
        )

    refs = (part, sbuf, (rq, rp, rm), (r1p, r1m, r1q))
    far = Scatter(place, 1 - place.zh, product, refs, ss.at[0], rs.at[0])
    near = Scatter(place, place.zh, product, refs, ss.at[1], rs.at[1])
    far.open()
    near.open()
    far.turn()
    near.turn()
    far.close()
    out = remote(sbuf.at[place.own, 1 - place.zh], rz, zs.at[3], zr.at[3], place.partner())
    out.start()
    near.close()
    out.wait_recv()
    dnormed = part[place.own, place.zh] + rz[...].astype(F32)
    scaled = dnormed * gain_cols
    dtrans_out[...] = trans_scale * (scaled - trans_ref[...] * pull)
    out.wait_send()
    for copy in far.sent + near.sent:
        copy.wait_send()
    for copy in (cross_x, cross_t, cross_l):
        copy.wait_send()
    for steps in planes:
        steps.drain()
    table.drain()
    pool.drain()
    x_copy.wait()


def last_kernel(x, dtrans, kl, grad, grad_bias, kl_mean):
    rounded = dtrans[...].astype(BF16)
    for k in range(4):
        for zh in (0, 1):
            v = zh * 4 + k
            grad[v * FB : (v + 1) * FB, :] = lax.dot_general(
                x[k, zh], rounded, (((1,), (0,)), ((), ())), preferred_element_type=F32
            ).astype(BF16)

    @pl.when(pl.program_id(0) == 0)
    def _():
        grad_bias[...] = jnp.sum(dtrans[...], axis=0, keepdims=True)
        kl_mean[0] = jnp.sum(kl[...]) / ROWS


def per_device(hidden, final_hidden, row_pick, trans_weight, trans_bias, norm_gain, unembed):
    whole = pl.BlockSpec(memory_space=pltpu.VMEM)
    anywhere = pl.BlockSpec(memory_space=pl.ANY)
    dma = pltpu.SemaphoreType.DMA
    shape = jax.ShapeDtypeStruct
    block = pltpu.VMEM((16, 2, ROWS, FB), BF16)
    x_all, dtrans, kl = pl.pallas_call(
        kernel,
        name="lens",
        out_shape=(shape((16, 2, FB, ROWS), BF16), shape((ROWS, FB), F32), shape((1, ROWS), F32)),
        in_specs=[whole, anywhere, anywhere, anywhere, whole, whole, anywhere],
        out_specs=(anywhere, whole, whole),
        scratch_shapes=[
            pltpu.VMEM((POOL, FB), BF16),
            block,
            pltpu.VMEM((16, 2, FB, ROWS), BF16),
            pltpu.VMEM((16, 2, 2 * ROWS, FB), BF16),
            pltpu.VMEM((NS, POOL // NS, FB), BF16),
            pltpu.VMEM((D, FB), BF16),
            pltpu.VMEM((NS, SHARD, VOC), BF16),
            pltpu.VMEM((ROWS, FB), F32),
            pltpu.VMEM((2 * ROWS, VOC), F32),
            pltpu.VMEM((NV, 8, 128), F32),
            pltpu.VMEM((NV, 8, 128), F32),
            pltpu.VMEM((16, 2, ROWS, FB), F32),
            block,
            block,
            block,
            block,
            pltpu.VMEM((2, ROWS, FB), BF16),
            pltpu.VMEM((2, ROWS, FB), BF16),
            pltpu.VMEM((2, ROWS, FB), BF16),
            pltpu.VMEM((ROWS, FB), BF16),
            dma((3,)),
            dma,
            dma,
            dma((2, 4, CHUNKS)),
            dma((4, CHUNKS)),
            dma((NS, CHUNKS)),
            dma((4,)),
            dma((4,)),
            dma((NS,)),
            pltpu.SemaphoreType.REGULAR((5, 2)),
            dma((4,)),
            dma((4,)),
            dma((6, N_MSG)),
            dma((6, N_MSG)),
        ]
        + [dma((2, N_MSG))] * 2
        + [dma((NV,))] * 4,
        compiler_params=pltpu.CompilerParams(
            collective_id=0, has_side_effects=True, vmem_limit_bytes=VMEM_LIMIT
        ),
    )(row_pick, hidden[0], final_hidden, trans_weight[0], trans_bias, norm_gain, unembed)
    grad_weight, grad_bias, kl_mean = pl.pallas_call(
        last_kernel,
        name="weight_gradient",
        grid=(4,),
        out_shape=(shape((D, FB), BF16), shape((1, FB), F32), shape((1,), F32)),
        in_specs=[
            pl.BlockSpec((4, 2, FB, ROWS), lambda y: (y, 0, 0, 0)),
            pl.BlockSpec((ROWS, FB), lambda y: (0, 0)),
            pl.BlockSpec((1, ROWS), lambda y: (0, 0)),
        ],
        out_specs=(
            pl.BlockSpec((D // 4, FB), lambda y: (y, 0)),
            pl.BlockSpec((1, FB), lambda y: (0, 0)),
            pl.BlockSpec(memory_space=pltpu.SMEM),
        ),
    )(x_all, dtrans, kl)
    return grad_weight[None], grad_bias, kl_mean


def solution(mesh):
    placed = (
        P("section", None, "vocab"),
        P("section", "vocab"),
        P("section", None),
        P("section", None, "vocab"),
        P("section", "vocab"),
        P("vocab"),
        P("section", "vocab"),
    )
    return jax.shard_map(
        per_device,
        mesh=mesh,
        in_specs=placed,
        out_specs=(P("section", None, "vocab"), P("section", "vocab"), P("section")),
        check_vma=False,
    )
```

```python
import jax
import jax.numpy as jnp
from jax import lax
from jax.experimental import pallas as pl
from jax.experimental.pallas import tpu as pltpu
from jax.sharding import PartitionSpec as P

MESH = pl.DeviceIdType.MESH
F32, BF16 = jnp.float32, jnp.bfloat16
EPS = 1e-05
NV, NS = 32, 8
ROWS, POOL, D, VOC, FB = 128, 512, 8192, 512, 256
VMEM_LIMIT = 60 * 1024 * 1024
N_MSG = 30
STEPS = (1, -1, 2)
CHUNKS = 4
SHARD = D // NS
PIECE = SHARD // CHUNKS


def vid(y, x, zh):
    return y * 8 + zh * 4 + x


def ring(a, c):
    return lax.rem(a + (c + 4), 4)


class Place:
    def __init__(self):
        self.v = lax.axis_index("vocab")
        self.s = lax.axis_index("section")
        self.x = lax.rem(self.v, 4)
        self.zh = lax.rem(self.v // 4, 2)
        self.y = self.v // 8
        self.own = self.y * 4 + self.x

    def to(self, v):
        return (self.s, v)

    def partner(self):
        return self.to(vid(self.y, self.x, 1 - self.zh))

    def along_z(self, step):
        z = lax.rem(self.zh * 4 + self.s // 2 + (step + 8), 8)
        return (lax.rem(z, 4) * 2 + lax.rem(self.s, 2), vid(self.y, self.x, z // 4))

    def touching(self):
        across = (self.s + 1 - 2 * lax.rem(self.s, 2), self.v)
        sides = [self.near(half, 1, step) for half in (0, 1) for step in (1, -1)]
        return sides + [self.along_z(1), self.along_z(-1), across]

    def near(self, half, stage, step):
        along_x = (half == 0) == (stage == 1)
        if along_x:
            return self.to(vid(self.y, ring(self.x, step), self.zh))
        return self.to(vid(ring(self.y, step), self.x, self.zh))

    def pair(self, half, c, d):
        if half == 0:
            return ring(self.y, d) * 4 + ring(self.x, c)
        return ring(self.y, c) * 4 + ring(self.x, d)


def remote(src, dst, send_sem, recv_sem, device):
    return pltpu.make_async_remote_copy(
        src_ref=src, dst_ref=dst, send_sem=send_sem, recv_sem=recv_sem, device_id=device, device_id_type=MESH
    )


def announce(place):
    barrier = pltpu.get_barrier_semaphore()
    for device in place.touching():
        pl.semaphore_signal(barrier, inc=1, device_id=device, device_id_type=MESH)


def await_touching(place):
    pl.semaphore_wait(pltpu.get_barrier_semaphore(), len(place.touching()))


def widen_plane(place, known):
    for half in (0, 1):
        for side in (0, 1):
            pl.semaphore_signal(
                known.at[3 + half, side],
                inc=1,
                device_id=place.near(half, 1, 1 - 2 * side),
                device_id_type=MESH,
            )
    for half in (0, 1):
        for side in (0, 1):
            pl.semaphore_wait(known.at[3 + half, side], 1)


def widen(place, known, turn):
    for side in (0, 1):
        pl.semaphore_signal(
            known.at[turn, side], inc=1, device_id=place.along_z(1 - 2 * side), device_id_type=MESH
        )
    for side in (0, 1):
        pl.semaphore_wait(known.at[turn, side], 1)


def send_stats(place, stats, send_sem, recv_sem):
    @pl.loop(1, NV)
    def _(k):
        remote(
            stats.at[place.v],
            stats.at[place.v],
            send_sem.at[k],
            recv_sem.at[place.v],
            place.to(lax.rem(place.v + k, NV)),
        ).start()


def wait_stats(place, stats, send_sem, recv_sem):
    @pl.loop(1, NV)
    def _(k):
        src = lax.rem(place.v + k, NV)
        copy = remote(stats.at[src], stats.at[src], send_sem.at[k], recv_sem.at[src], place.to(src))
        copy.wait_send()
        copy.wait_recv()


def to_lanes(columns):
    lane = lax.broadcasted_iota(jnp.int32, (ROWS, 128), 1)
    tile = jnp.zeros((ROWS, 128), F32)
    for k, column in enumerate(columns):
        tile = jnp.where(lane == k, column, tile)
    return tile.T[0:8, :]


def to_columns(tile):
    return jnp.concatenate([tile, jnp.zeros((120, 128), F32)], axis=0).T


class Plane:
    def __init__(self, place, buf, level, base, send_sem, recv_sem):
        self.place, self.buf, self.level, self.base = place, buf, level, base
        self.ss, self.rs = send_sem, recv_sem
        self.sent = []
        self.ids = {}

    def move(self, name, pair, half, device):
        rows = pl.ds(self.base + half * (ROWS // 2), ROWS // 2)
        ref = self.buf.at[pair, self.level, rows, :]
        k = self.ids.setdefault(name, len(self.ids))
        return remote(ref, ref, self.ss.at[k], self.rs.at[k], device)

    def first(self, half, c):
        p = self.place
        self.sent.append(self.move((half, c), p.own, half, p.near(half, 1, c)))
        self.sent[-1].start()

    def second(self, half, c, d):
        p = self.place
        self.sent.append(self.move((half, c, d), p.pair(half, -c, 0), half, p.near(half, 2, d)))
        self.sent[-1].start()

    def steps(self):
        p = self.place
        for c in STEPS:
            for half in (0, 1):
                self.first(half, c)
        for d in STEPS:
            for half in (0, 1):
                self.second(half, 0, d)
        yield
        for c in STEPS:
            for half in (0, 1):
                self.move((half, c), p.pair(half, -c, 0), half, p.near(half, 1, -c)).wait_recv()
                for d in STEPS:
                    self.second(half, c, d)
            yield
        for c in (0,) + STEPS:
            for half in (0, 1):
                for d in STEPS:
                    self.move((half, c, d), p.pair(half, -c, -d), half, p.near(half, 2, -d)).wait_recv()
        yield

    def drain(self):
        for copy in self.sent:
            copy.wait_send()


class Scatter:
    def __init__(self, place, level, product, refs, send_sem, recv_sem):
        self.place, self.level, self.product = place, level, product
        self.part, self.sbuf, self.arrive, self.last = refs
        self.ss, self.rs = send_sem, recv_sem
        self.sent = []
        self.ids = {}

    def rows(self, half):
        return pl.ds(half * (ROWS // 2), ROWS // 2)

    def landing(self, name, pair):
        if len(name) == 3:
            return self.arrive[STEPS.index(name[2])].at[pair, self.level, self.rows(name[0]), :]
        return self.last[STEPS.index(name[1])].at[self.level, self.rows(name[0]), :]

    def move(self, name, src, dst, device):
        k = self.ids.setdefault(name, len(self.ids))
        return remote(src, dst, self.ss.at[k], self.rs.at[k], device)

    def send(self, name, pair, device, value):
        half = name[0]
        self.sbuf[pair, self.level, self.rows(half), :] = value.astype(BF16)
        src = self.sbuf.at[pair, self.level, self.rows(half), :]
        self.sent.append(self.move(name, src, self.landing(name, pair), device))
        self.sent[-1].start()

    def receive(self, name, pair, device):
        ref = self.landing(name, pair)
        self.move(name, ref, ref, device).wait_recv()
        return ref[...].astype(F32)

    def mine(self, half, c, d):
        return self.part[self.place.pair(half, c, d), self.level, self.rows(half), :]

    def open(self):
        p = self.place
        order = [(a, b) for a in (2, 1, -1) for b in (2, 1, -1)]
        order += [(a, 0) for a in (2, 1, -1)] + [(0, b) for b in (2, 1, -1)] + [(0, 0)]
        for dx, dy in order:
            pair = p.pair(0, dx, dy)
            self.product(pair, self.level)
            for half in (0, 1):
                c, d = (dx, dy) if half == 0 else (dy, dx)
                if d != 0:
                    self.send((half, c, d), pair, p.near(half, 2, d), self.mine(half, c, d))

    def column(self, half, c):
        p = self.place
        total = self.mine(half, c, 0)
        for d in STEPS:
            total = total + self.receive((half, c, d), p.pair(half, c, 0), p.near(half, 2, -d))
        return total

    def turn(self):
        p = self.place
        for c in (2, 1, -1):
            for half in (0, 1):
                self.send((half, c), p.pair(half, c, 0), p.near(half, 1, c), self.column(half, c))

    def close(self):
        p = self.place
        for half in (0, 1):
            total = self.column(half, 0)
            for c in STEPS:
                total = total + self.receive((half, c), p.own, p.near(half, 1, -c))
            self.sbuf[p.own, self.level, self.rows(half), :] = total.astype(BF16)
            self.part[p.own, self.level, self.rows(half), :] = total


class Table:
    def __init__(self, place, mine, buf, to_z, to_core, arrived, local):
        self.place, self.mine, self.buf = place, mine, buf
        self.to_z, self.to_core, self.arrived, self.local = to_z, to_core, arrived, local
        self.core = lax.rem(place.s, 2)
        self.zl = place.s // 2

    def piece(self, shard, part):
        return self.buf.at[shard, pl.ds(part * PIECE, PIECE), :]

    def along(self, i, part, sign, src=None):
        shard = 2 * i + self.core
        here = self.piece(shard, part) if src is None else src
        return remote(
            here,
            self.piece(shard, part),
            self.to_z.at[0 if sign > 0 else 1, i, part],
            self.arrived.at[shard, part],
            (self.place.s + 2 * sign, self.place.v),
        )

    def across(self, i, part, src=None):
        shard = 2 * i + self.core
        here = self.piece(shard, part) if src is None else src
        return remote(
            here,
            self.piece(shard, part),
            self.to_core.at[i, part],
            self.arrived.at[shard, part],
            (self.place.s + 1 - 2 * self.core, self.place.v),
        )

    def start(self, parts):
        for part in parts:
            src = self.mine.at[pl.ds(part * PIECE, PIECE), :]

            @pl.when(self.zl < 3)
            def _():
                self.along(self.zl, part, 1, src).start()

            @pl.when(self.zl > 0)
            def _():
                self.along(self.zl, part, -1, src).start()

            self.across(self.zl, part, src).start()

    def wait(self, shard, part):
        ref = self.piece(shard, part)
        remote(ref, ref, self.to_core.at[0, part], self.arrived.at[shard, part], (self.place.s, self.place.v)).wait_recv()

    def relay(self, wave, part):
        for side in (-1, 1):
            i = self.zl + side * wave
            beyond = self.zl - side

            @pl.when((i >= 0) & (i <= 3))
            def _():
                self.wait(2 * i + self.core, part)

                @pl.when((beyond >= 0) & (beyond <= 3))
                def _():
                    self.along(i, part, -side).start()

                self.across(i, part).start()

    def drain(self):
        for part in range(CHUNKS):
            for i in range(4):

                @pl.when((self.zl < 3) & (self.zl >= i))
                def _():
                    self.along(i, part, 1).wait_send()

                @pl.when((self.zl > 0) & (self.zl <= i))
                def _():
                    self.along(i, part, -1).wait_send()

                self.across(i, part).wait_send()


class Finals:
    def __init__(self, place, mine, buf, to_z, to_core, arrived):
        self.place, self.mine, self.buf = place, mine, buf
        self.to_z, self.to_core, self.arrived = to_z, to_core, arrived
        self.core = lax.rem(place.s, 2)
        self.zl = place.s // 2

    def along(self, k):
        i = lax.rem(self.zl + k, 4)
        return remote(
            self.mine,
            self.buf.at[self.place.s],
            self.to_z.at[k],
            self.arrived.at[self.place.s],
            (2 * i + self.core, self.place.v),
        )

    def across(self, k):
        shard = 2 * lax.rem(self.zl + k, 4) + self.core
        here = self.mine if k == 0 else self.buf.at[shard]
        return remote(
            here,
            self.buf.at[shard],
            self.to_core.at[k],
            self.arrived.at[shard],
            (self.place.s + 1 - 2 * self.core, self.place.v),
        )

    def wait(self, shard):
        ref = self.buf.at[shard]
        remote(ref, ref, self.to_core.at[0], self.arrived.at[shard], (self.place.s, self.place.v)).wait_recv()

    def start(self):
        for k in (1, 2, 3):
            self.along(k).start()
        self.across(0).start()

    def forward(self):
        for k in (1, 2, 3):
            self.wait(2 * lax.rem(self.zl + k, 4) + self.core)
            self.across(k).start()

    def finish(self):
        for k in range(4):
            self.wait(2 * lax.rem(self.zl + k, 4) + 1 - self.core)

    def drain(self):
        for k in (1, 2, 3):
            self.along(k).wait_send()
        for k in range(4):
            self.across(k).wait_send()


def kernel(
    pick, hidden_hbm, final_hbm, w_hbm, bias, gain, u_mine, x_out, dtrans_out, kl_out,
    hidden, xbuf, xt, lt, fbuf, wbuf, u, trans_ref, acc, scale_stats, stats, part, sbuf, rq, rp, rm, r1p, r1m, r1q, rz,
    in_sem, x_sem, u_sem, uz, uc, ua, fz, fc, fa, known, zs, zr, pss, prs, ss, rs, sts1, str1, sts2, str2,
):
    place = Place()
    announce(place)
    table = Table(place, u_mine, u, uz, uc, ua, u_sem)
    pool = Finals(place, final_hbm, fbuf, fz, fc, fa)
    hidden_copy = pltpu.make_async_copy(hidden_hbm, hidden, in_sem.at[0])
    hidden_copy.start()
    final_copy = pltpu.make_async_copy(final_hbm, fbuf.at[place.s], in_sem.at[1])
    final_copy.start()
    w_copy = pltpu.make_async_copy(w_hbm, wbuf, in_sem.at[2])
    w_copy.start()
    chosen = jnp.broadcast_to(pick[...].astype(F32), (ROWS, ROWS)).T[:, 0:1].astype(jnp.int32)
    onehot = jnp.where(lax.broadcasted_iota(jnp.int32, (ROWS, POOL), 1) == chosen, 1.0, 0.0).astype(BF16)
    gain_cols = gain[...].astype(F32).reshape(1, FB)

    planes = []

    def plane(buf, level, base):
        k = len(planes)
        planes.append(Plane(place, buf, level, base, pss.at[k], prs.at[k]))
        return planes[-1].steps()

    def go(steps, count=1):
        for _ in range(count):
            next(steps)

    def crossing(buf, base, k, level):
        ref = buf.at[place.own, level, pl.ds(base, ROWS), :]
        return remote(ref, ref, zs.at[k], zr.at[k], place.partner())

    near_x, far_x = plane(xbuf, place.zh, 0), plane(xbuf, 1 - place.zh, 0)
    near_t, far_t = plane(lt, place.zh, ROWS), plane(lt, 1 - place.zh, ROWS)
    near_l, far_l = plane(lt, place.zh, 0), plane(lt, 1 - place.zh, 0)

    def multiply(level):
        @pl.loop(0, 4)
        def _(y):
            total = trans_ref[...]
            for x in range(4):
                rows = pl.ds(pl.multiple_of(vid(y, x, level) * FB, FB), FB)
                total = total + jnp.dot(xbuf[y * 4 + x, level], wbuf[rows, :], preferred_element_type=F32)
            trans_ref[...] = total

    await_touching(place)
    table.start((0, 1))
    hidden_copy.wait()
    inputs = jnp.dot(onehot, hidden[...], preferred_element_type=F32)
    xbuf[place.own, place.zh] = inputs.astype(BF16)
    trans_ref[...] = inputs + bias[...].astype(F32)
    widen_plane(place, known)
    go(near_x)
    widen(place, known, 0)
    go(near_x, 2)
    widen(place, known, 1)
    pool.start()
    go(near_x)
    widen(place, known, 2)
    cross_x = crossing(xbuf, 0, 0, place.zh)
    cross_x.start()
    table.start((2, 3))
    u_copy = pltpu.make_async_copy(u_mine, u.at[place.s], u_sem)
    u_copy.start()
    go(near_x)
    crossing(xbuf, 0, 0, 1 - place.zh).wait_recv()
    go(far_x)
    final_copy.wait()
    pool.forward()
    go(far_x, 3)
    table.relay(1, 0)
    pool.finish()
    finals = jnp.dot(onehot, fbuf[...].reshape(POOL, FB), preferred_element_type=F32)
    lt[place.own, place.zh, ROWS : 2 * ROWS] = (finals * gain_cols).astype(BF16)
    cross_t = crossing(lt, ROWS, 1, place.zh)
    cross_t.start()
    go(near_t)
    w_copy.wait()
    multiply(place.zh)
    table.relay(1, 1)
    go(near_t, 3)
    go(far_x)
    multiply(1 - place.zh)
    trans = trans_ref[...]
    lt[place.own, place.zh, 0:ROWS] = (trans * gain_cols).astype(BF16)
    cross_l = crossing(lt, 0, 2, place.zh)
    cross_l.start()
    go(near_l)
    scale_stats[place.v] = to_lanes(
        [jnp.sum(trans * trans, axis=1, keepdims=True), jnp.sum(finals * finals, axis=1, keepdims=True)]
    )
    send_stats(place, scale_stats, sts1, str1)
    table.relay(1, 2)
    go(near_l, 3)
    crossing(lt, ROWS, 1, 1 - place.zh).wait_recv()
    go(far_t)
    table.relay(1, 3)
    go(far_t, 3)
    crossing(lt, 0, 2, 1 - place.zh).wait_recv()
    go(far_l)
    table.relay(2, 0)
    go(far_l, 3)
    go(near_t)
    go(near_l)
    table.relay(2, 1)
    go(far_t)
    go(far_l)
    table.relay(2, 2)
    acc[...] = jnp.zeros_like(acc)

    def absorb(shard, first, count):
        total = acc[...]
        for k in range(first, first + count):
            total = total + jnp.dot(
                lt[(shard // 2) * 4 + k, lax.rem(shard, 2)],
                u[shard, k * FB : (k + 1) * FB, :],
                preferred_element_type=F32,
            )
        acc[...] = total

    def each_side(wave, then):
        for side in (-1, 1):
            i = table.zl + side * wave

            @pl.when((i >= 0) & (i <= 3))
            def _():
                then(2 * i + table.core, 2 * i + 1 - table.core)

    def absorb_pair(own, other):
        absorb(own, 0, 4)
        for piece in range(CHUNKS):
            table.wait(other, piece)
        absorb(other, 0, 4)

    u_copy.wait()
    absorb_pair(place.s, place.s + 1 - 2 * table.core)
    each_side(1, absorb_pair)
    table.relay(2, 3)
    each_side(2, absorb_pair)

    @pl.loop(0, 16)
    def _(p):
        for zh in (0, 1):
            xt[p, zh] = xbuf[p, zh].astype(F32).T.astype(BF16)

    x_copy = pltpu.make_async_copy(xt, x_out, x_sem)
    x_copy.start()
    for piece in range(CHUNKS):
        table.relay(3, piece)

        def absorb_piece(own, other):
            absorb(own, piece, 1)
            table.wait(other, piece)
            absorb(other, piece, 1)

        each_side(3, absorb_piece)
    wait_stats(place, scale_stats, sts1, str1)
    scale = lax.rsqrt(jnp.sum(scale_stats[...], axis=0) / D + EPS)


    columns = to_columns(scale)
    trans_scale, final_scale = columns[:, 0:1], columns[:, 1:2]
    logits = acc[0:ROWS] * trans_scale
    target = acc[ROWS : 2 * ROWS] * final_scale

    def totals(values):
        highest = jnp.max(values, axis=1, keepdims=True)
        shifted = values - highest
        weights = jnp.exp(shifted)
        return highest, shifted, weights, jnp.sum(weights, axis=1, keepdims=True)

    l_max, l_shift, l_exp, l_sum = totals(logits)
    t_max, t_shift, t_exp, t_sum = totals(target)
    stats[place.v] = to_lanes(
        [
            l_max,
            l_sum,
            jnp.sum(l_exp * l_shift, axis=1, keepdims=True),
            t_max,
            t_sum,
            jnp.sum(t_exp * t_shift, axis=1, keepdims=True),
            jnp.sum(t_exp * l_shift, axis=1, keepdims=True),
        ]
    )
    send_stats(place, stats, sts2, str2)
    wait_stats(place, stats, sts2, str2)
    lm, ls, la, tm, ts, ta, tb = (stats[:, k, :] for k in range(7))

    def over(values):
        return jnp.sum(values, axis=0, keepdims=True)

    l_top = jnp.max(lm, axis=0, keepdims=True)
    t_top = jnp.max(tm, axis=0, keepdims=True)
    lw, tw = jnp.exp(lm - l_top), jnp.exp(tm - t_top)
    l_total, t_total = over(lw * ls), over(tw * ts)
    mean_l = over(lw * (la + ls * (lm - l_top))) / l_total
    mean_t = over(tw * (ta + ts * (tm - t_top))) / t_total
    mean_tl = over(tw * (tb + ts * (lm - l_top))) / t_total
    kl_rows = mean_t - mean_tl - jnp.log(t_total) + jnp.log(l_total)
    kl_out[...] = kl_rows
    l_norm = l_top + jnp.log(l_total)
    t_norm = t_top + jnp.log(t_total)
    pull = scale[0:1, :] * (mean_l - mean_tl) / D
    columns = to_columns(jnp.concatenate([l_norm, t_norm, pull, jnp.zeros((5, 128), F32)], axis=0))
    l_norm, t_norm, pull = columns[:, 0:1], columns[:, 1:2], columns[:, 2:3]
    dlogits = (jnp.exp(logits - l_norm) - jnp.exp(target - t_norm)).astype(BF16)

    def product(pair, level):
        y, x = pair // 4, lax.rem(pair, 4)
        rows = pl.ds(pl.multiple_of(x * FB, FB), FB)
        part[pair, level] = lax.dot_general(
            dlogits, u[2 * y + level, rows, :], (((1,), (1,)), ((), ())), preferred_element_type=F32
        )

    refs = (part, sbuf, (rq, rp, rm), (r1p, r1m, r1q))
    far = Scatter(place, 1 - place.zh, product, refs, ss.at[0], rs.at[0])
    near = Scatter(place, place.zh, product, refs, ss.at[1], rs.at[1])
    far.open()
    far.turn()
    near.open()
    far.close()
    out = remote(sbuf.at[place.own, 1 - place.zh], rz, zs.at[3], zr.at[3], place.partner())
    out.start()
    near.turn()
    near.close()
    out.wait_recv()
    dnormed = part[place.own, place.zh] + rz[...].astype(F32)
    scaled = dnormed * gain_cols
    dtrans_out[...] = trans_scale * (scaled - trans_ref[...] * pull)
    out.wait_send()
    for copy in far.sent + near.sent:
        copy.wait_send()
    for copy in (cross_x, cross_t, cross_l):
        copy.wait_send()
    for steps in planes:
        steps.drain()
    table.drain()
    pool.drain()
    x_copy.wait()


def last_kernel(x, dtrans, kl, grad, grad_bias, kl_mean):
    rounded = dtrans[...].astype(BF16)
    for k in range(8):
        for zh in (0, 1):
            v = (k // 4) * 8 + zh * 4 + k % 4
            grad[v * FB : (v + 1) * FB, :] = lax.dot_general(
                x[k, zh], rounded, (((1,), (0,)), ((), ())), preferred_element_type=F32
            ).astype(BF16)

    @pl.when(pl.program_id(0) == 0)
    def _():
        grad_bias[...] = jnp.sum(dtrans[...], axis=0, keepdims=True)
        kl_mean[0] = jnp.sum(kl[...]) / ROWS


def per_device(hidden, final_hidden, row_pick, trans_weight, trans_bias, norm_gain, unembed):
    whole = pl.BlockSpec(memory_space=pltpu.VMEM)
    anywhere = pl.BlockSpec(memory_space=pl.ANY)
    dma = pltpu.SemaphoreType.DMA
    shape = jax.ShapeDtypeStruct
    block = pltpu.VMEM((16, 2, ROWS, FB), BF16)
    x_all, dtrans, kl = pl.pallas_call(
        kernel,
        name="lens",
        out_shape=(shape((16, 2, FB, ROWS), BF16), shape((ROWS, FB), F32), shape((1, ROWS), F32)),
        in_specs=[whole, anywhere, anywhere, anywhere, whole, whole, anywhere],
        out_specs=(anywhere, whole, whole),
        scratch_shapes=[
            pltpu.VMEM((POOL, FB), BF16),
            block,
            pltpu.VMEM((16, 2, FB, ROWS), BF16),
            pltpu.VMEM((16, 2, 2 * ROWS, FB), BF16),
            pltpu.VMEM((NS, POOL // NS, FB), BF16),
            pltpu.VMEM((D, FB), BF16),
            pltpu.VMEM((NS, SHARD, VOC), BF16),
            pltpu.VMEM((ROWS, FB), F32),
            pltpu.VMEM((2 * ROWS, VOC), F32),
            pltpu.VMEM((NV, 8, 128), F32),
            pltpu.VMEM((NV, 8, 128), F32),
            pltpu.VMEM((16, 2, ROWS, FB), F32),
            block,
            block,
            block,
            block,
            pltpu.VMEM((2, ROWS, FB), BF16),
            pltpu.VMEM((2, ROWS, FB), BF16),
            pltpu.VMEM((2, ROWS, FB), BF16),
            pltpu.VMEM((ROWS, FB), BF16),
            dma((3,)),
            dma,
            dma,
            dma((2, 4, CHUNKS)),
            dma((4, CHUNKS)),
            dma((NS, CHUNKS)),
            dma((4,)),
            dma((4,)),
            dma((NS,)),
            pltpu.SemaphoreType.REGULAR((5, 2)),
            dma((4,)),
            dma((4,)),
            dma((6, N_MSG)),
            dma((6, N_MSG)),
        ]
        + [dma((2, N_MSG))] * 2
        + [dma((NV,))] * 4,
        compiler_params=pltpu.CompilerParams(
            collective_id=0, has_side_effects=True, vmem_limit_bytes=VMEM_LIMIT
        ),
    )(row_pick, hidden[0], final_hidden, trans_weight[0], trans_bias, norm_gain, unembed)
    grad_weight, grad_bias, kl_mean = pl.pallas_call(
        last_kernel,
        name="weight_gradient",
        grid=(2,),
        out_shape=(shape((D, FB), BF16), shape((1, FB), F32), shape((1,), F32)),
        in_specs=[
            pl.BlockSpec((8, 2, FB, ROWS), lambda y: (y, 0, 0, 0)),
            pl.BlockSpec((ROWS, FB), lambda y: (0, 0)),
            pl.BlockSpec((1, ROWS), lambda y: (0, 0)),
        ],
        out_specs=(
            pl.BlockSpec((D // 2, FB), lambda y: (y, 0)),
            pl.BlockSpec((1, FB), lambda y: (0, 0)),
            pl.BlockSpec(memory_space=pltpu.SMEM),
        ),
    )(x_all, dtrans, kl)
    return grad_weight[None], grad_bias, kl_mean


def solution(mesh):
    placed = (
        P("section", None, "vocab"),
        P("section", "vocab"),
        P("section", None),
        P("section", None, "vocab"),
        P("section", "vocab"),
        P("vocab"),
        P("section", "vocab"),
    )
    return jax.shard_map(
        per_device,
        mesh=mesh,
        in_specs=placed,
        out_specs=(P("section", None, "vocab"), P("section", "vocab"), P("section")),
        check_vma=False,
    )
```
